128 devices in a mesh: wide: 16 (over y, x), narrow: 8 (over z, core).
Axes of the slice: x: 4, y: 4, z: 4, core: 2. Of those that a mesh axis runs over, the one named last changes fastest.
Arguments:
- diag_block: float32 [256, 256], P('narrow'), as said below
- panel_below: float32 [24576, 256], P(('wide', 'narrow')), may hold values from -0.216 to 0.216
- trailing_slab: float32 [12288, 24576], P('narrow', 'wide'), may hold values from -6 to 6
Outputs:
- updated: float32 [12288, 24576], P('narrow', 'wide')
The draws below stay inside these ranges and needn't reach their ends.
Inputs may be any that keep to these rules, and one draw needn't show every extreme that they name: `diag_block`: symmetric positive definite; its smallest eigenvalue is 0.01 or more and its diagonal entries lie between 0.4 and 2.1.
All inputs are finite; a program needn't handle non-finite values.
Results may differ from the reference program's by a relative error of at most 0.00016.
Values sent between devices are 32-bit elements; how exact they have to be, the bound alone decides.
A program may use at most 64 MiB of HBM per device.

```python
import jax
import jax.numpy as jnp
from jax import lax

NB = 256
K = 24576
M = 12288


def draw_diag_block(key, part):
    key_time = jax.random.fold_in(key, 11)
    key_scale = jax.random.fold_in(key, 12)
    key_noise = jax.random.fold_in(key, 13)
    key_period = jax.random.fold_in(key, 14)
    offsets = jax.random.uniform(key_time, (NB,), jnp.float32, 0.0, 0.5)
    times = jnp.arange(NB).astype(jnp.float32) + offsets
    distance = jnp.abs(times[:, None] - times[None, :])
    period_len = NB * jax.random.uniform(key_period, (), jnp.float32, 0.16, 0.25)
    chord = period_len / jnp.pi * jnp.abs(jnp.sin(jnp.pi * distance / period_len))
    seasonal = jnp.exp(-distance / NB) * jnp.exp(-chord / 4.0)
    kernel = 0.35 * jnp.exp(-distance / 6.0) + 0.65 * seasonal
    log_scales = jax.random.uniform(key_scale, (NB,), jnp.float32, -0.35667494, 0.33647224)
    scales = jnp.exp(log_scales)
    noise = jax.random.uniform(key_noise, (NB,), jnp.float32, 0.01, 0.03)
    outer = scales[:, None] * scales[None, :]
    identity = jnp.eye(NB, dtype=jnp.float32)
    return kernel * outer + identity * noise[:, None]


def steps_of(own_key, dims, pieces, smallest, top_value):
    level = 1.0
    for position, parts in pieces:
        draws = jax.random.uniform(jax.random.fold_in(jax.random.fold_in(own_key, 6), position), (parts,), jnp.float32, smallest / len(pieces), top_value / len(pieces))
        level = level * jnp.repeat(jnp.exp(draws), dims[position] // parts).reshape((-1,) + (1,) * (len(dims) - 1 - position))
    return level


def gaussian(own_key, shape, spread, most, pieces=(), held_as=jnp.bfloat16):
    values = spread * jax.random.normal(own_key, shape, jnp.float32)
    if pieces:
        values = values * steps_of(own_key, shape, pieces, -0.22, 0.18)
    return jnp.clip(values, -most, most).astype(held_as)


def setup_inputs(seed: int = 0) -> dict:
    streams_of = jax.random.split(jax.random.key(seed), 4)
    return {
        "diag_block": draw_diag_block(jax.random.fold_in(streams_of[3], 71), 0),
        "panel_below": gaussian(streams_of[1], (K, NB), 0.036, 0.216, ((0, 128),), jnp.float32),
        "trailing_slab": gaussian(streams_of[2], (M, K), 1.0, 6.0, ((0, 8), (1, 16)), jnp.float32),
    }


unit_gamma = 65538.0 * 2.0 ** (-24) / (1.0 - 65538.0 * 2.0 ** (-24))

def factor_block(diag_full):
    trace_sum = jnp.sum(jnp.diagonal(diag_full))
    shift_value = unit_gamma * trace_sum / diag_full.shape[0]
    identity = jnp.eye(diag_full.shape[0], dtype=jnp.float32)
    return jnp.linalg.cholesky(diag_full - shift_value * identity)

def solve_rows(raw_panel, lower_factor):
    return jax.scipy.linalg.solve_triangular(lower_factor, raw_panel.T, lower=True).T

def reference(diag_block, panel_below, trailing_slab):
    lower_factor = factor_block(diag_block)
    panel_rows = solve_rows(panel_below, lower_factor)
    slab_panel = panel_rows[:trailing_slab.shape[0]]
    product = lax.dot_general(slab_panel.astype(jnp.float32), panel_rows.astype(jnp.float32), (((1,), (1,)), ((), ())), precision=lax.Precision.HIGHEST, preferred_element_type=jnp.float32)
    return trailing_slab - product
```

```python
import functools

import jax
import jax.numpy as jnp
from jax import lax
from jax.experimental import pallas as pl
from jax.experimental.pallas import tpu as pltpu
from jax.sharding import PartitionSpec as P

unit_gamma = 65538.0 * 2.0 ** (-24) / (1.0 - 65538.0 * 2.0 ** (-24))
MESH = pl.DeviceIdType.MESH
LAST = (((1,), (1,)), ((), ()))
PLAIN = (((1,), (0,)), ((), ()))


def full_dot(a, b, dims):
    return lax.dot_general(
        a, b, dims, precision=lax.Precision.HIGHEST, preferred_element_type=jnp.float32
    )


def half_dot(a, b, dims):
    return lax.dot_general(a, b, dims, preferred_element_type=jnp.float32)


def halves(x):
    high = x.astype(jnp.bfloat16)
    low = (x - high.astype(jnp.float32)).astype(jnp.bfloat16)
    return high, low


def eliminate(m_ref, out_ref):
    count = 16
    lane = lax.broadcasted_iota(jnp.int32, (8, 128), 1)
    sub = lax.broadcasted_iota(jnp.int32, (8, 128), 0)
    blocks = [m_ref[8 * i : 8 * i + 8, :] for i in range(count)]
    for j in range(count):
        first = 8 * j
        block = blocks[j]
        inside = (lane >= first) & (lane < first + 8)
        a, e = {}, {}
        for q in range(8):
            column = jnp.broadcast_to(block[:, first + q : first + q + 1], (8, 128))
            for p in range(q, 8):
                a[p, q] = jnp.broadcast_to(column[p : p + 1, :], (8, 128))
        eye = (lane - first == sub).astype(jnp.float32)
        placed = jnp.where(inside, eye, block)
        lead = [jnp.broadcast_to(placed[m : m + 1, :], (8, 128)) for m in range(8)]
        inverse = [None] * 8
        for k in range(8):
            inverse[k] = 1.0 / a[k, k]
            for i in range(k + 1, 8):
                factor = a[i, k] * inverse[k]
                for q in range(k + 1, i + 1):
                    a[i, q] = a[i, q] - factor * a[q, k]
                lead[i] = lead[i] - factor * lead[k]
                for q in range(k):
                    e[i, q] = e[i, q] - factor * e[k, q]
                e[i, k] = -factor
        scaled = [inverse[m] * lead[m] for m in range(8)]
        solved = list(scaled)
        for m in range(8):
            for n in range(m + 1, 8):
                solved[m] = solved[m] + e[n, m] * scaled[n]
        rows = lead[0] * lax.rsqrt(a[0, 0])
        for m in range(1, 8):
            rows = jnp.where(sub == m, lead[m] * lax.rsqrt(a[m, m]), rows)
        out_ref[first : first + 8, :] = jnp.where(lane <= sub + first, rows, 0.0)
        for i in range(j + 1, count):
            below = blocks[i]
            total = jnp.where(inside, 0.0, below)
            for m in range(8):
                weight = jnp.broadcast_to(below[:, first + m : first + m + 1], (8, 128))
                total = total - weight * solved[m]
            blocks[i] = total


def gather_kernel(
    diag_ref, panel_ref, row_ref, col_ref,
    diag_all, col_all, row_all, work, inv,
    diag_send, diag_recv, col_send, col_recv, part_send, part_recv, row_send, row_recv,
):
    w, n = lax.axis_index("wide"), lax.axis_index("narrow")
    wides, narrows = 16, 8
    part = panel_ref.shape[0] // 2
    piece = lax.rem(w + 12, wides)
    source = (n, lax.div(piece, 2))
    barrier = pltpu.get_barrier_semaphore()

    def target(half):
        return (lax.rem(2 * n + half + 4, wides), w)

    def signal(device):
        pl.semaphore_signal(barrier, inc=1, device_id=device, device_id_type=MESH)

    for step in range(1, narrows):
        signal((w, lax.rem(n + step, narrows)))
    for step in range(1, wides):
        signal((lax.rem(w + step, wides), n))
    signal(source)

    @pl.when(w < narrows)
    def _():
        signal(target(0))
        signal(target(1))

    diag_all[n] = diag_ref[...]
    col_all[n] = panel_ref[...]
    peers = narrows + wides - 1

    @pl.when(w < narrows)
    def _():
        pl.semaphore_wait(barrier, peers + 2)

    @pl.when(w >= narrows)
    def _():
        pl.semaphore_wait(barrier, peers)

    def diag_copy(step):
        return pltpu.make_async_remote_copy(
            diag_ref, diag_all.at[n], diag_send.at[step], diag_recv.at[step],
            device_id=(w, lax.rem(n + step, narrows)), device_id_type=MESH)

    def col_copy(step):
        return pltpu.make_async_remote_copy(
            panel_ref, col_all.at[n], col_send.at[step], col_recv.at[step],
            device_id=(w, lax.rem(n + step, narrows)), device_id_type=MESH)

    def part_copy(half):
        return pltpu.make_async_remote_copy(
            panel_ref.at[pl.ds(part * half, part)], row_all.at[2 * n + half],
            part_send.at[half], part_recv.at[0],
            device_id=target(half), device_id_type=MESH)

    def row_copy(step):
        return pltpu.make_async_remote_copy(
            row_all.at[piece], row_all.at[piece], row_send.at[step], row_recv.at[step],
            device_id=(lax.rem(w + step, wides), n), device_id_type=MESH)

    for step in range(1, narrows):
        diag_copy(step).start()

    @pl.when(w < narrows)
    def _():
        part_copy(0).start()
        part_copy(1).start()

    for step in range(1, narrows):
        col_copy(step).start()
    part_copy(0).wait_recv()
    for step in range(1, wides):
        row_copy(step).start()
    for step in range(1, narrows):
        diag_copy(step).wait_recv()

    row_id = lax.broadcasted_iota(jnp.int32, (32, 256), 0)
    col_id = lax.broadcasted_iota(jnp.int32, (32, 256), 1)
    trace = jnp.zeros((32, 256), jnp.float32)
    for i in range(narrows):
        trace = trace + jnp.where(col_id == row_id + 32 * i, diag_all[i], 0.0)
    shift = unit_gamma * jnp.sum(trace, keepdims=True) / 256.0
    for i in range(narrows):
        work[32 * i : 32 * i + 32, :] = jnp.where(
            col_id == row_id + 32 * i, diag_all[i] - shift, diag_all[i])
    eliminate(work.at[0:128, 0:128], inv.at[0:128, 0:128])
    inv[0:128, 128:256] = jnp.zeros((128, 128), jnp.float32)
    first = inv[0:128, 0:128]
    below = full_dot(work[128:256, 0:128], first, LAST)
    beside = full_dot(first, work[0:128, 128:256], PLAIN)
    work[128:256, 128:256] = work[128:256, 128:256] - full_dot(below, beside, PLAIN)
    eliminate(work.at[128:256, 128:256], inv.at[128:256, 128:256])
    inv[128:256, 0:128] = -full_dot(
        inv[128:256, 128:256], full_dot(below, first, PLAIN), PLAIN)

    inv_high, inv_low = halves(inv[...])

    def solve(raw, out_ref, start):
        high, low = halves(raw)
        done = (half_dot(high, inv_high, LAST) + half_dot(high, inv_low, LAST)
                + half_dot(low, inv_high, LAST))
        high, low = halves(done)
        out_ref[pl.ds(start, raw.shape[0]), 0:256] = high
        out_ref[pl.ds(start, raw.shape[0]), 256:512] = low

    for step in range(1, narrows):
        col_copy(step).wait_recv()

    @pl.loop(0, narrows)
    def _(i):
        solve(col_all[i], col_ref, pl.multiple_of(i * 192, 192))

    for step in range(1, wides):
        row_copy(step).wait_recv()

    @pl.loop(0, wides)
    def _(i):
        solve(row_all[i], row_ref, pl.multiple_of(i * 96, 96))

    for step in range(1, narrows):
        diag_copy(step).wait_send()
        col_copy(step).wait_send()
    for step in range(1, wides):
        row_copy(step).wait_send()

    @pl.when(w < narrows)
    def _():
        part_copy(0).wait_send()
        part_copy(1).wait_send()


def gather_and_solve(diag_block, panel_below):
    rows = panel_below.shape[0]
    vmem = pl.BlockSpec(memory_space=pltpu.VMEM)
    out = jax.ShapeDtypeStruct((8 * rows, 512), jnp.bfloat16)
    sems = pltpu.SemaphoreType.DMA
    return pl.pallas_call(
        gather_kernel,
        out_shape=(out, out),
        in_specs=[vmem, vmem],
        out_specs=(vmem, vmem),
        scratch_shapes=[
            pltpu.VMEM((8, 32, 256), jnp.float32),
            pltpu.VMEM((8, rows, 256), jnp.float32),
            pltpu.VMEM((16, rows // 2, 256), jnp.float32),
            pltpu.VMEM((256, 256), jnp.float32),
            pltpu.VMEM((256, 256), jnp.float32),
            sems((8,)), sems((8,)), sems((8,)), sems((8,)),
            sems((2,)), sems((1,)), sems((16,)), sems((16,)),
        ],
        compiler_params=pltpu.CompilerParams(
            collective_id=0, has_side_effects=True, vmem_limit_bytes=24 << 20),
        name="gather_and_solve",
    )(diag_block, panel_below)


def update_kernel(row_ref, col_ref, slab_ref, out_ref):
    high, low = row_ref[:, 0:256], row_ref[:, 256:512]
    col_high, col_low = col_ref[:, 0:256], col_ref[:, 256:512]
    product = (half_dot(high, col_high, LAST) + half_dot(high, col_low, LAST)
               + half_dot(low, col_high, LAST))
    out_ref[...] = slab_ref[...] - product


def update(row_panel, col_panel, slab):
    rows, cols = slab.shape
    tile = 256
    return pl.pallas_call(
        update_kernel,
        out_shape=jax.ShapeDtypeStruct(slab.shape, jnp.float32),
        grid=(rows // tile,),
        in_specs=[
            pl.BlockSpec((tile, 512), lambda i: (i, 0)),
            pl.BlockSpec((cols, 512), lambda i: (0, 0)),
            pl.BlockSpec((tile, cols), lambda i: (i, 0)),
        ],
        out_specs=pl.BlockSpec((tile, cols), lambda i: (i, 0)),
        compiler_params=pltpu.CompilerParams(vmem_limit_bytes=32 << 20),
        name="update",
    )(row_panel, col_panel, slab)


def on_device(diag_block, panel_below, trailing_slab):
    row_panel, col_panel = gather_and_solve(diag_block, panel_below)
    return update(row_panel, col_panel, trailing_slab)


def solution(mesh):
    placed = (P("narrow", None), P(("wide", "narrow"), None), P("narrow", "wide"))
    return jax.shard_map(
        on_device, mesh=mesh, in_specs=placed, out_specs=P("narrow", "wide"), check_vma=False
    )
```

```python
import functools

import jax
import jax.numpy as jnp
from jax import lax
from jax.experimental import pallas as pl
from jax.experimental.pallas import tpu as pltpu
from jax.sharding import PartitionSpec as P

unit_gamma = 65538.0 * 2.0 ** (-24) / (1.0 - 65538.0 * 2.0 ** (-24))
MESH = pl.DeviceIdType.MESH
PHASE_TWO, TWIN = 6, 4
LAST = (((1,), (1,)), ((), ()))
PLAIN = (((1,), (0,)), ((), ()))


def full_dot(a, b, dims):
    return lax.dot_general(
        a, b, dims, precision=lax.Precision.HIGHEST, preferred_element_type=jnp.float32
    )


def half_dot(a, b, dims):
    return lax.dot_general(a, b, dims, preferred_element_type=jnp.float32)


def halves(x):
    high = x.astype(jnp.bfloat16)
    low = (x - high.astype(jnp.float32)).astype(jnp.bfloat16)
    return high, low


def eliminate(m_ref, out_ref, errands=None):
    count = 16
    lane = lax.broadcasted_iota(jnp.int32, (8, 128), 1)
    sub = lax.broadcasted_iota(jnp.int32, (8, 128), 0)
    blocks = [m_ref[8 * i : 8 * i + 8, :] for i in range(count)]
    for j in range(count):
        if errands and j in errands:
            errands[j]()
        first = 8 * j
        block = blocks[j]
        inside = (lane >= first) & (lane < first + 8)
        a, e = {}, {}
        for q in range(8):
            column = jnp.broadcast_to(block[:, first + q : first + q + 1], (8, 128))
            for p in range(q, 8):
                a[p, q] = jnp.broadcast_to(column[p : p + 1, :], (8, 128))
        eye = (lane - first == sub).astype(jnp.float32)
        placed = jnp.where(inside, eye, block)
        lead = [jnp.broadcast_to(placed[m : m + 1, :], (8, 128)) for m in range(8)]
        inverse = [None] * 8
        for k in range(8):
            inverse[k] = 1.0 / a[k, k]
            for i in range(k + 1, 8):
                factor = a[i, k] * inverse[k]
                for q in range(k + 1, i + 1):
                    a[i, q] = a[i, q] - factor * a[q, k]
                lead[i] = lead[i] - factor * lead[k]
                for q in range(k):
                    e[i, q] = e[i, q] - factor * e[k, q]
                e[i, k] = -factor
        scaled = [inverse[m] * lead[m] for m in range(8)]
        solved = list(scaled)
        for m in range(8):
            for n in range(m + 1, 8):
                solved[m] = solved[m] + e[n, m] * scaled[n]
        rows = lead[0] * lax.rsqrt(a[0, 0])
        for m in range(1, 8):
            rows = jnp.where(sub == m, lead[m] * lax.rsqrt(a[m, m]), rows)
        out_ref[first : first + 8, :] = jnp.where(lane <= sub + first, rows, 0.0)
        for i in range(j + 1, count):
            below = blocks[i]
            total = jnp.where(inside, 0.0, below)
            for m in range(8):
                weight = jnp.broadcast_to(below[:, first + m : first + m + 1], (8, 128))
                total = total - weight * solved[m]
            blocks[i] = total


def gather_kernel(
    diag_hbm, panel_hbm, slab_hbm, row_ref, col_ref, slab_ref,
    diag_all, traces, col_all, row_a, row_b, work, inv,
    local_sem, diag_send, diag_recv, rest_send, rest_recv, col_send, col_recv,
    twin_send, twin_recv, part_send, part_recv, one_send, one_recv, two_send, two_recv,
):
    w, n = lax.axis_index("wide"), lax.axis_index("narrow")
    y, x = lax.div(w, 4), lax.rem(w, 4)
    z, core = lax.div(n, 2), lax.rem(n, 2)
    piece = lax.rem(w + 12, 16)
    piece_y, piece_x = lax.div(piece, 4), lax.rem(piece, 4)
    slot_a, slot_b = 4 * piece_y + piece_x, 4 * piece_x + piece_y
    twin = (w, 2 * z + 1 - core)

    def along_x(step):
        return (4 * y + lax.rem(x + step, 4), n)

    def along_y(step):
        return (4 * lax.rem(y + step, 4) + x, n)

    def along_z(step):
        return (w, 2 * lax.rem(z + step, 4) + core)

    def target(half):
        return (lax.rem(2 * n + half + 4, 16), w)

    source = (n, lax.div(piece, 2))

    slab_copy = pltpu.make_async_copy(slab_hbm, slab_ref, local_sem.at[0])
    diag_own = pltpu.make_async_copy(
        diag_hbm, diag_all.at[pl.ds(pl.multiple_of(32 * n, 32), 32)], local_sem.at[1])
    panel_own = pltpu.make_async_copy(
        panel_hbm, col_all.at[pl.ds(pl.multiple_of(192 * n, 64), 192)], local_sem.at[2])
    diag_own.start()
    panel_own.start()

    barrier = pltpu.get_barrier_semaphore()

    def signal(device):
        pl.semaphore_signal(barrier, inc=1, device_id=device, device_id_type=MESH)

    for step in range(1, 8):
        signal((w, lax.rem(n + step, 8)))
    for step in range(1, 4):
        signal(along_x(step))
        signal(along_y(step))
    signal(source)

    @pl.when(w < 8)
    def _():
        signal(target(0))
        signal(target(1))

    slab_copy.start()
    diag_own.wait()
    row_id = lax.broadcasted_iota(jnp.int32, (32, 256), 0)
    col_id = lax.broadcasted_iota(jnp.int32, (32, 256), 1)
    own = diag_all[pl.ds(pl.multiple_of(32 * n, 32), 32), :]
    own = jnp.where(col_id == row_id + 32 * n, own, 0.0)
    own = own[:, 0:128] + own[:, 128:256]
    traces[n] = jnp.sum(own, axis=0, keepdims=True)

    @pl.when(w < 8)
    def _():
        pl.semaphore_wait(barrier, 16)

    @pl.when(w >= 8)
    def _():
        pl.semaphore_wait(barrier, 14)

    def remote(src, dst, send, recv, device):
        return pltpu.make_async_remote_copy(
            src, dst, send, recv, device_id=device, device_id_type=MESH)

    def corner_copy(step, origin):
        block = diag_all.at[pl.ds(pl.multiple_of(32 * origin, 32), 32), 0:128]
        return remote(block, block, diag_send.at[step], diag_recv.at[origin],
                      (w, lax.rem(n + step, 8)))

    def trace_copy(step, origin):
        return remote(traces.at[origin], traces.at[origin], diag_send.at[step],
                      diag_recv.at[origin], (w, lax.rem(n + step, 8)))

    def rest_copy(step, origin):
        block = diag_all.at[pl.ds(pl.multiple_of(32 * origin, 32), 32)]
        return remote(block, block, rest_send.at[step], rest_recv.at[origin],
                      (w, lax.rem(n + step, 8)))

    def part_copy(half, side):
        p = 2 * n + half
        p_y, p_x = lax.div(p, 4), lax.rem(p, 4)
        place = 48 * (4 * p_x + p_y if side else 4 * p_y + p_x)
        return remote(
            col_all.at[pl.ds(pl.multiple_of(192 * n + 96 * half + 48 * side, 48), 48)],
            (row_b if side else row_a).at[pl.ds(pl.multiple_of(place, 48), 48)],
            part_send.at[2 * half + side], part_recv.at[side], target(half))

    def one_copy(step, side):
        buffer, slot = (row_b, slot_b) if side else (row_a, slot_a)
        block = buffer.at[pl.ds(pl.multiple_of(48 * slot, 48), 48)]
        return remote(block, block, one_send.at[side, step], one_recv.at[side, step],
                      along_y(step) if side else along_x(step))

    def two_copy(step, side):
        buffer, slot = (row_b, piece_x) if side else (row_a, piece_y)
        block = buffer.at[pl.ds(pl.multiple_of(192 * slot, 192), 192)]
        return remote(block, block, two_send.at[side, step], two_recv.at[side, step],
                      along_x(step) if side else along_y(step))

    def col_copy(step):
        block = col_all.at[pl.ds(pl.multiple_of(192 * n, 64), 192)]
        return remote(block, block, col_send.at[step], col_recv.at[step], along_z(step))

    def twin_copy(step):
        origin = 2 * lax.rem(z + 4 - step, 4) + core
        block = col_all.at[pl.ds(pl.multiple_of(192 * origin, 64), 192)]
        return remote(block, block, twin_send.at[step], twin_recv.at[step], twin)

    @pl.when(n < 4)
    def _():
        for step in range(1, 8):
            corner_copy(step, n).start()

    @pl.when(n >= 4)
    def _():
        for step in range(1, 8):
            trace_copy(step, n).start()

    panel_own.wait()

    @pl.when(w < 8)
    def _():
        for half in range(2):
            for side in range(2):
                part_copy(half, side).start()

    @pl.when(n >= 4)
    def _():
        for step in range(1, 8):
            rest_copy(step, n).start()

    for side in range(2):
        part_copy(0, side).wait_recv()
    for step in range(1, 4):
        one_copy(step, 0).start()
        one_copy(step, 1).start()
    for step in range(1, 4):
        col_copy(step).start()
    twin_copy(0).start()

    for origin in range(4):
        @pl.when(n != origin)
        def _():
            corner_copy(1, origin).wait_recv()
    for origin in range(4, 8):
        @pl.when(n != origin)
        def _():
            trace_copy(1, origin).wait_recv()

    total = jnp.zeros((8, 128), jnp.float32)
    sub = lax.broadcasted_iota(jnp.int32, (8, 128), 0)
    lane = lax.broadcasted_iota(jnp.int32, (8, 128), 1)
    for i in range(16):
        total = total + jnp.where(lane == sub + 8 * i, diag_all[8 * i : 8 * i + 8, 0:128], 0.0)
    total = jnp.sum(total, axis=0, keepdims=True)
    for i in range(4, 8):
        total = total + traces[i]
    shift = unit_gamma * jnp.sum(total, axis=1, keepdims=True) / 256.0

    def shifted(start):
        for i in range(16):
            block = diag_all[start + 8 * i : start + 8 * i + 8, start : start + 128]
            work[start + 8 * i : start + 8 * i + 8, :] = jnp.where(
                lane == sub + 8 * i, block - shift, block)

    def second_phase():
        for side in range(2):
            for step in range(1, 4):
                one_copy(step, side).wait_recv()
        for step in range(1, 4):
            two_copy(step, 0).start()
            two_copy(step, 1).start()

    def to_twin():
        for step in range(1, 4):
            col_copy(step).wait_recv()
            twin_copy(step).start()

    shifted(0)
    eliminate(work.at[0:128], inv.at[0:128, 0:128], {PHASE_TWO: second_phase})
    inv[0:128, 128:256] = jnp.zeros((128, 128), jnp.float32)
    for origin in range(4, 8):
        @pl.when(n != origin)
        def _():
            rest_copy(1, origin).wait_recv()
    shifted(128)
    first = inv[0:128, 0:128]
    corner = diag_all[128:256, 0:128]
    below = full_dot(corner, first, LAST)
    beside = full_dot(first, corner, LAST)
    work[128:256, :] = work[128:256, :] - full_dot(below, beside, PLAIN)
    eliminate(work.at[128:256], inv.at[128:256, 128:256], {TWIN: to_twin})
    inv[128:256, 0:128] = -full_dot(
        inv[128:256, 128:256], full_dot(below, first, PLAIN), PLAIN)

    inv_high, inv_low = halves(inv[...])

    def solve(raw):
        high, low = halves(raw)
        return halves(half_dot(high, inv_high, LAST) + half_dot(high, inv_low, LAST)
                      + half_dot(low, inv_high, LAST))

    for step in range(4):
        twin_copy(step).wait_recv()
    for start in (0, 768):
        high, low = solve(col_all[start : start + 768, :])
        col_ref[start : start + 768, 0:256] = high
        col_ref[start : start + 768, 256:512] = low
    for side in range(2):
        for step in range(1, 4):
            two_copy(step, side).wait_recv()
        high, low = solve((row_b if side else row_a)[...])
        for slot in range(16):
            place = 96 * (4 * (slot % 4) + slot // 4) + 48 if side else 96 * slot
            row_ref[place : place + 48, 0:256] = high[48 * slot : 48 * slot + 48]
            row_ref[place : place + 48, 256:512] = low[48 * slot : 48 * slot + 48]

    @pl.when(n < 4)
    def _():
        for step in range(1, 8):
            corner_copy(step, n).wait_send()

    @pl.when(n >= 4)
    def _():
        for step in range(1, 8):
            trace_copy(step, n).wait_send()
            rest_copy(step, n).wait_send()

    @pl.when(w < 8)
    def _():
        for half in range(2):
            for side in range(2):
                part_copy(half, side).wait_send()

    for step in range(1, 4):
        for side in range(2):
            one_copy(step, side).wait_send()
            two_copy(step, side).wait_send()
        col_copy(step).wait_send()
    for step in range(4):
        twin_copy(step).wait_send()
    slab_copy.wait()


def gather_and_solve(diag_block, panel_below, slab):
    rows = panel_below.shape[0]
    vmem = pl.BlockSpec(memory_space=pltpu.VMEM)
    hbm = pl.BlockSpec(memory_space=pltpu.HBM)
    out = jax.ShapeDtypeStruct((8 * rows, 512), jnp.bfloat16)
    sems = pltpu.SemaphoreType.DMA
    return pl.pallas_call(
        gather_kernel,
        out_shape=(out, out, jax.ShapeDtypeStruct(slab.shape, slab.dtype)),
        in_specs=[hbm, hbm, hbm],
        out_specs=(vmem, vmem, vmem),
        scratch_shapes=[
            pltpu.VMEM((256, 256), jnp.float32),
            pltpu.VMEM((8, 1, 128), jnp.float32),
            pltpu.VMEM((8 * rows, 256), jnp.float32),
            pltpu.VMEM((4 * rows, 256), jnp.float32),
            pltpu.VMEM((4 * rows, 256), jnp.float32),
            pltpu.VMEM((256, 128), jnp.float32),
            pltpu.VMEM((256, 256), jnp.float32),
            sems((3,)), sems((8,)), sems((8,)), sems((8,)), sems((8,)), sems((4,)), sems((4,)),
            sems((4,)), sems((4,)), sems((4,)), sems((2,)), sems((2, 4)), sems((2, 4)),
            sems((2, 4)), sems((2, 4)),
        ],
        compiler_params=pltpu.CompilerParams(
            collective_id=0, has_side_effects=True, vmem_limit_bytes=28 << 20),
        name="gather_and_solve",
    )(*(pltpu.with_memory_space_constraint(a, pltpu.HBM) for a in (diag_block, panel_below, slab)))


def update_kernel(row_ref, col_ref, slab_ref, out_hbm, buffer, sem):
    rows, cols = slab_ref.shape
    tall, broad, depth = 768, 512, 3
    tiles = [(i, j) for i in range(0, rows, tall) for j in range(0, cols, broad)]

    def out_copy(t):
        i, j = tiles[t]
        return pltpu.make_async_copy(
            buffer.at[t % depth], out_hbm.at[pl.ds(i, tall), pl.ds(j, broad)], sem.at[t % depth])

    for t, (i, j) in enumerate(tiles):
        if t >= depth:
            out_copy(t - depth).wait()
        high, low = row_ref[i : i + tall, 0:256], row_ref[i : i + tall, 256:512]
        col_high, col_low = col_ref[j : j + broad, 0:256], col_ref[j : j + broad, 256:512]
        product = (half_dot(high, col_high, LAST) + half_dot(high, col_low, LAST)
                   + half_dot(low, col_high, LAST))
        buffer[t % depth] = slab_ref[i : i + tall, j : j + broad] - product
        out_copy(t).start()
    for t in range(len(tiles) - depth, len(tiles)):
        out_copy(t).wait()


def update(row_panel, col_panel, slab):
    vmem = pl.BlockSpec(memory_space=pltpu.VMEM)
    return pl.pallas_call(
        update_kernel,
        out_shape=jax.ShapeDtypeStruct(slab.shape, jnp.float32),
        in_specs=[vmem, vmem, vmem],
        out_specs=pl.BlockSpec(memory_space=pltpu.HBM),
        scratch_shapes=[pltpu.VMEM((3, 768, 512), jnp.float32), pltpu.SemaphoreType.DMA((3,))],
        compiler_params=pltpu.CompilerParams(vmem_limit_bytes=24 << 20),
        name="update",
    )(row_panel, col_panel, slab)


def on_device(diag_block, panel_below, trailing_slab):
    row_panel, col_panel, slab = gather_and_solve(diag_block, panel_below, trailing_slab)
    return update(row_panel, col_panel, slab)


def solution(mesh):
    placed = (P("narrow", None), P(("wide", "narrow"), None), P("narrow", "wide"))
    return jax.shard_map(
        on_device, mesh=mesh, in_specs=placed, out_specs=P("narrow", "wide"), check_vma=False
    )
```

```python
import functools

import jax
import jax.numpy as jnp
from jax import lax
from jax.experimental import pallas as pl
from jax.experimental.pallas import tpu as pltpu
from jax.sharding import PartitionSpec as P

unit_gamma = 65538.0 * 2.0 ** (-24) / (1.0 - 65538.0 * 2.0 ** (-24))
MESH = pl.DeviceIdType.MESH
PHASE_TWO, PHASE_THREE, TWIN, COLS_FIRST = 6, 4, 8, False
LAST = (((1,), (1,)), ((), ()))
PLAIN = (((1,), (0,)), ((), ()))


def full_dot(a, b, dims):
    return lax.dot_general(
        a, b, dims, precision=lax.Precision.HIGHEST, preferred_element_type=jnp.float32
    )


def half_dot(a, b, dims):
    return lax.dot_general(a, b, dims, preferred_element_type=jnp.float32)


def halves(x):
    high = x.astype(jnp.bfloat16)
    low = (x - high.astype(jnp.float32)).astype(jnp.bfloat16)
    return high, low


def eliminate(m_ref, out_ref, errands=None):
    count = 16
    lane = lax.broadcasted_iota(jnp.int32, (8, 128), 1)
    sub = lax.broadcasted_iota(jnp.int32, (8, 128), 0)
    blocks = [m_ref[8 * i : 8 * i + 8, :] for i in range(count)]
    for j in range(count):
        if errands and j in errands:
            errands[j]()
        first = 8 * j
        block = blocks[j]
        inside = (lane >= first) & (lane < first + 8)
        a, e = {}, {}
        for q in range(8):
            column = jnp.broadcast_to(block[:, first + q : first + q + 1], (8, 128))
            for p in range(q, 8):
                a[p, q] = jnp.broadcast_to(column[p : p + 1, :], (8, 128))
        eye = (lane - first == sub).astype(jnp.float32)
        placed = jnp.where(inside, eye, block)
        lead = [jnp.broadcast_to(placed[m : m + 1, :], (8, 128)) for m in range(8)]
        inverse = [None] * 8
        for k in range(8):
            inverse[k] = 1.0 / a[k, k]
            for i in range(k + 1, 8):
                factor = a[i, k] * inverse[k]
                for q in range(k + 1, i + 1):
                    a[i, q] = a[i, q] - factor * a[q, k]
                lead[i] = lead[i] - factor * lead[k]
                for q in range(k):
                    e[i, q] = e[i, q] - factor * e[k, q]
                e[i, k] = -factor
        scaled = [inverse[m] * lead[m] for m in range(8)]
        solved = list(scaled)
        for m in range(8):
            for n in range(m + 1, 8):
                solved[m] = solved[m] + e[n, m] * scaled[n]
        rows = lead[0] * lax.rsqrt(a[0, 0])
        for m in range(1, 8):
            rows = jnp.where(sub == m, lead[m] * lax.rsqrt(a[m, m]), rows)
        out_ref[first : first + 8, :] = jnp.where(lane <= sub + first, rows, 0.0)
        for i in range(j + 1, count):
            below = blocks[i]
            total = jnp.where(inside, 0.0, below)
            for m in range(8):
                weight = jnp.broadcast_to(below[:, first + m : first + m + 1], (8, 128))
                total = total - weight * solved[m]
            blocks[i] = total


def gather_kernel(
    diag_hbm, panel_hbm, slab_hbm, row_ref, col_ref, slab_ref,
    diag_all, traces, col_all, row_a, row_b, work, inv,
    local_sem, diag_send, diag_recv, rest_send, rest_recv, col_send, col_recv,
    twin_send, twin_recv, part_send, part_recv, one_send, one_recv, two_send, two_recv,
    relay_send, relay_recv,
):
    w, n = lax.axis_index("wide"), lax.axis_index("narrow")
    y, x = lax.div(w, 4), lax.rem(w, 4)
    z, core = lax.div(n, 2), lax.rem(n, 2)

    def piece_at(col, row):
        dx, dy = lax.rem(col + 4 - lax.rem(n, 4), 4), lax.rem(row + 4 - lax.div(n, 4), 4)
        return 4 * lax.rem(dx + dy + z + 2, 4) + dy

    ahead = 1 + 2 * core
    twin = (w, 2 * z + 1 - core)

    def along_x(step):
        return (4 * y + lax.rem(x + step, 4), n)

    def along_y(step):
        return (4 * lax.rem(y + step, 4) + x, n)

    def along_z(step):
        return (w, 2 * lax.rem(z + step, 4) + core)

    def target(half):
        dy = 2 * core + half
        dx = lax.rem(z + 10 - dy - lax.div(w, 2), 4)
        return (4 * lax.rem(y + dy, 4) + lax.rem(x + dx, 4), w)

    source = (n, lax.div(piece_at(x, y), 2))

    slab_copy = pltpu.make_async_copy(slab_hbm, slab_ref, local_sem.at[0])
    diag_own = pltpu.make_async_copy(
        diag_hbm, diag_all.at[pl.ds(pl.multiple_of(32 * n, 32), 32)], local_sem.at[1])
    panel_own = pltpu.make_async_copy(
        panel_hbm, col_all.at[pl.ds(pl.multiple_of(192 * n, 64), 192)], local_sem.at[2])
    diag_own.start()
    panel_own.start()

    barrier = pltpu.get_barrier_semaphore()

    def signal(device):
        pl.semaphore_signal(barrier, inc=1, device_id=device, device_id_type=MESH)

    for step in range(1, 8):
        signal((w, lax.rem(n + step, 8)))
    for step in range(1, 4):
        signal(along_x(step))
        signal(along_y(step))
    signal(source)

    @pl.when(w < 8)
    def _():
        signal(target(0))
        signal(target(1))

    slab_copy.start()
    diag_own.wait()
    row_id = lax.broadcasted_iota(jnp.int32, (32, 256), 0)
    col_id = lax.broadcasted_iota(jnp.int32, (32, 256), 1)
    own = diag_all[pl.ds(pl.multiple_of(32 * n, 32), 32), :]
    own = jnp.where(col_id == row_id + 32 * n, own, 0.0)
    own = own[:, 0:128] + own[:, 128:256]
    traces[n] = jnp.sum(own, axis=0, keepdims=True)

    @pl.when(w < 8)
    def _():
        pl.semaphore_wait(barrier, 16)

    @pl.when(w >= 8)
    def _():
        pl.semaphore_wait(barrier, 14)

    def remote(src, dst, send, recv, device):
        return pltpu.make_async_remote_copy(
            src, dst, send, recv, device_id=device, device_id_type=MESH)

    def corner_copy(step, origin):
        block = diag_all.at[pl.ds(pl.multiple_of(32 * origin, 32), 32), 0:128]
        return remote(block, block, diag_send.at[step], diag_recv.at[origin],
                      (w, lax.rem(n + step, 8)))

    def trace_copy(step, origin):
        return remote(traces.at[origin], traces.at[origin], diag_send.at[step],
                      diag_recv.at[origin], (w, lax.rem(n + step, 8)))

    def rest_copy(step, origin):
        block = diag_all.at[pl.ds(pl.multiple_of(32 * origin, 32), 32)]
        return remote(block, block, rest_send.at[step], rest_recv.at[origin],
                      (w, lax.rem(n + step, 8)))

    line = (y, x)

    def pieces(side, row, first, count):
        start = 192 * row + 48 * first
        return (row_b if side else row_a).at[pl.ds(pl.multiple_of(start, 48), 48 * count)]

    def part_copy(half, side):
        row = lax.rem(target(half)[0], 4) if side else lax.div(target(half)[0], 4)
        return remote(
            col_all.at[pl.ds(pl.multiple_of(192 * n + 96 * half + 48 * side, 48), 48)],
            pieces(side, row, 0, 1), part_send.at[2 * half + side], part_recv.at[side],
            target(half))

    def one_copy(step, side):
        return remote(
            pieces(side, line[side], 0, 1), pieces(side, line[side], 4 - step, 1),
            one_send.at[side, step], one_recv.at[side, step],
            along_y(step) if side else along_x(step))

    def across(step, side):
        return along_x(step) if side else along_y(step)

    def two_copy(step, side, rest):
        block = pieces(side, line[side], 1, 3) if rest else pieces(side, line[side], 0, 1)
        return remote(block, block, two_send.at[side, rest, step], two_recv.at[side, rest, step],
                      across(step, side))

    def relay_copy(side, rest):
        row = lax.rem(line[side] + 4 - ahead, 4)
        block = pieces(side, row, 1, 3) if rest else pieces(side, row, 0, 1)
        return remote(block, block, relay_send.at[side, rest], relay_recv.at[side, rest],
                      across(ahead, side))

    def wait_two(side, rest, forward):
        @pl.when(core == (0 if forward else 1))
        def _():
            two_copy(1, side, rest).wait_recv()

        @pl.when(core == (1 if forward else 0))
        def _():
            two_copy(3, side, rest).wait_recv()

    def col_copy(step):
        block = col_all.at[pl.ds(pl.multiple_of(192 * n, 64), 192)]
        return remote(block, block, col_send.at[step], col_recv.at[step], along_z(step))

    def twin_copy(step):
        origin = 2 * lax.rem(z + 4 - step, 4) + core
        block = col_all.at[pl.ds(pl.multiple_of(192 * origin, 64), 192)]
        return remote(block, block, twin_send.at[step], twin_recv.at[step], twin)

    @pl.when(n < 4)
    def _():
        for step in range(1, 8):
            corner_copy(step, n).start()

    @pl.when(n >= 4)
    def _():
        for step in range(1, 8):
            trace_copy(step, n).start()

    panel_own.wait()

    @pl.when(w < 8)
    def _():
        for half in range(2):
            for side in range(2):
                part_copy(half, side).start()

    @pl.when(n >= 4)
    def _():
        for step in range(1, 8):
            rest_copy(step, n).start()

    def start_cols():
        for step in (1, 3, 2):
            col_copy(step).start()
        twin_copy(0).start()

    def first_phase():
        for side in range(2):
            part_copy(0, side).wait_recv()
            for step in (1, 3, 2):
                one_copy(step, side).start()
            for step in (1, 3):
                two_copy(step, side, 0).start()

    if COLS_FIRST:
        start_cols()
        first_phase()
    else:
        first_phase()
        start_cols()

    for origin in range(4):
        @pl.when(n != origin)
        def _():
            corner_copy(1, origin).wait_recv()
    for origin in range(4, 8):
        @pl.when(n != origin)
        def _():
            trace_copy(1, origin).wait_recv()

    total = jnp.zeros((8, 128), jnp.float32)
    sub = lax.broadcasted_iota(jnp.int32, (8, 128), 0)
    lane = lax.broadcasted_iota(jnp.int32, (8, 128), 1)
    for i in range(16):
        total = total + jnp.where(lane == sub + 8 * i, diag_all[8 * i : 8 * i + 8, 0:128], 0.0)
    total = jnp.sum(total, axis=0, keepdims=True)
    for i in range(4, 8):
        total = total + traces[i]
    shift = unit_gamma * jnp.sum(total, axis=1, keepdims=True) / 256.0

    def shifted(start):
        for i in range(16):
            block = diag_all[start + 8 * i : start + 8 * i + 8, start : start + 128]
            work[start + 8 * i : start + 8 * i + 8, :] = jnp.where(
                lane == sub + 8 * i, block - shift, block)

    def second_phase():
        for side in range(2):
            for step in range(1, 4):
                one_copy(step, side).wait_recv()
            for step in (1, 3):
                two_copy(step, side, 1).start()
            wait_two(side, 0, True)
            relay_copy(side, 0).start()

    def third_phase():
        for side in range(2):
            wait_two(side, 1, True)
            relay_copy(side, 1).start()

    def to_twin():
        for step in range(1, 4):
            col_copy(step).wait_recv()
            twin_copy(step).start()

    shifted(0)
    eliminate(work.at[0:128], inv.at[0:128, 0:128], {PHASE_TWO: second_phase})
    inv[0:128, 128:256] = jnp.zeros((128, 128), jnp.float32)
    for origin in range(4, 8):
        @pl.when(n != origin)
        def _():
            rest_copy(1, origin).wait_recv()
    shifted(128)
    first = inv[0:128, 0:128]
    corner = diag_all[128:256, 0:128]
    below = full_dot(corner, first, LAST)
    beside = full_dot(first, corner, LAST)
    work[128:256, :] = work[128:256, :] - full_dot(below, beside, PLAIN)
    eliminate(work.at[128:256], inv.at[128:256, 128:256], {PHASE_THREE: third_phase, TWIN: to_twin})
    inv[128:256, 0:128] = -full_dot(
        inv[128:256, 128:256], full_dot(below, first, PLAIN), PLAIN)

    inv_high, inv_low = halves(inv[...])

    def solve(raw):
        high, low = halves(raw)
        return halves(half_dot(high, inv_high, LAST) + half_dot(high, inv_low, LAST)
                      + half_dot(low, inv_high, LAST))

    for step in range(4):
        twin_copy(step).wait_recv()
    for start in (0, 768):
        high, low = solve(col_all[start : start + 768, :])
        col_ref[start : start + 768, 0:256] = high
        col_ref[start : start + 768, 256:512] = low
    for side in range(2):
        wait_two(side, 0, False)
        wait_two(side, 1, False)
        relay_copy(side, 0).wait_recv()
        relay_copy(side, 1).wait_recv()
        high, low = solve((row_b if side else row_a)[...])
        for slot in range(16):
            row, other = slot // 4, lax.rem(line[1 - side] + slot % 4, 4)
            place = 96 * (piece_at(row, other) if side else piece_at(other, row)) + 48 * side
            place = pl.ds(pl.multiple_of(place, 48), 48)
            row_ref[place, 0:256] = high[48 * slot : 48 * slot + 48]
            row_ref[place, 256:512] = low[48 * slot : 48 * slot + 48]

    @pl.when(n < 4)
    def _():
        for step in range(1, 8):
            corner_copy(step, n).wait_send()

    @pl.when(n >= 4)
    def _():
        for step in range(1, 8):
            trace_copy(step, n).wait_send()
            rest_copy(step, n).wait_send()

    @pl.when(w < 8)
    def _():
        for half in range(2):
            for side in range(2):
                part_copy(half, side).wait_send()

    for side in range(2):
        for step in range(1, 4):
            one_copy(step, side).wait_send()
        for rest in range(2):
            two_copy(1, side, rest).wait_send()
            two_copy(3, side, rest).wait_send()
            relay_copy(side, rest).wait_send()
    for step in range(1, 4):
        col_copy(step).wait_send()
    for step in range(4):
        twin_copy(step).wait_send()
    slab_copy.wait()


def gather_and_solve(diag_block, panel_below, slab):
    rows = panel_below.shape[0]
    vmem = pl.BlockSpec(memory_space=pltpu.VMEM)
    hbm = pl.BlockSpec(memory_space=pltpu.HBM)
    out = jax.ShapeDtypeStruct((8 * rows, 512), jnp.bfloat16)
    sems = pltpu.SemaphoreType.DMA
    return pl.pallas_call(
        gather_kernel,
        out_shape=(out, out, jax.ShapeDtypeStruct(slab.shape, slab.dtype)),
        in_specs=[hbm, hbm, hbm],
        out_specs=(vmem, vmem, vmem),
        scratch_shapes=[
            pltpu.VMEM((256, 256), jnp.float32),
            pltpu.VMEM((8, 1, 128), jnp.float32),
            pltpu.VMEM((8 * rows, 256), jnp.float32),
            pltpu.VMEM((4 * rows, 256), jnp.float32),
            pltpu.VMEM((4 * rows, 256), jnp.float32),
            pltpu.VMEM((256, 128), jnp.float32),
            pltpu.VMEM((256, 256), jnp.float32),
            sems((3,)), sems((8,)), sems((8,)), sems((8,)), sems((8,)), sems((4,)), sems((4,)),
            sems((4,)), sems((4,)), sems((4,)), sems((2,)), sems((2, 4)), sems((2, 4)),
            sems((2, 2, 4)), sems((2, 2, 4)), sems((2, 2)), sems((2, 2)),
        ],
        compiler_params=pltpu.CompilerParams(
            collective_id=0, has_side_effects=True, vmem_limit_bytes=28 << 20),
        name="gather_and_solve",
    )(*(pltpu.with_memory_space_constraint(a, pltpu.HBM) for a in (diag_block, panel_below, slab)))


def update_kernel(row_ref, col_ref, slab_ref, out_hbm, buffer, sem):
    rows, cols = slab_ref.shape
    tall, broad, depth = 768, 512, 3
    tiles = [(i, j) for i in range(0, rows, tall) for j in range(0, cols, broad)]

    def out_copy(t):
        i, j = tiles[t]
        return pltpu.make_async_copy(
            buffer.at[t % depth], out_hbm.at[pl.ds(i, tall), pl.ds(j, broad)], sem.at[t % depth])

    for t, (i, j) in enumerate(tiles):
        if t >= depth:
            out_copy(t - depth).wait()
        high, low = row_ref[i : i + tall, 0:256], row_ref[i : i + tall, 256:512]
        col_high, col_low = col_ref[j : j + broad, 0:256], col_ref[j : j + broad, 256:512]
        product = (half_dot(high, col_high, LAST) + half_dot(high, col_low, LAST)
                   + half_dot(low, col_high, LAST))
        buffer[t % depth] = slab_ref[i : i + tall, j : j + broad] - product
        out_copy(t).start()
    for t in range(len(tiles) - depth, len(tiles)):
        out_copy(t).wait()


def update(row_panel, col_panel, slab):
    vmem = pl.BlockSpec(memory_space=pltpu.VMEM)
    return pl.pallas_call(
        update_kernel,
        out_shape=jax.ShapeDtypeStruct(slab.shape, jnp.float32),
        in_specs=[vmem, vmem, vmem],
        out_specs=pl.BlockSpec(memory_space=pltpu.HBM),
        scratch_shapes=[pltpu.VMEM((3, 768, 512), jnp.float32), pltpu.SemaphoreType.DMA((3,))],
        compiler_params=pltpu.CompilerParams(vmem_limit_bytes=24 << 20),
        name="update",
    )(row_panel, col_panel, slab)


def on_device(diag_block, panel_below, trailing_slab):
    row_panel, col_panel, slab = gather_and_solve(diag_block, panel_below, trailing_slab)
    return update(row_panel, col_panel, slab)


def solution(mesh):
    placed = (P("narrow", None), P(("wide", "narrow"), None), P("narrow", "wide"))
    return jax.shard_map(
        on_device, mesh=mesh, in_specs=placed, out_specs=P("narrow", "wide"), check_vma=False
    )
```

```python
import functools

import jax
import jax.numpy as jnp
from jax import lax
from jax.experimental import pallas as pl
from jax.experimental.pallas import tpu as pltpu
from jax.sharding import PartitionSpec as P

unit_gamma = 65538.0 * 2.0 ** (-24) / (1.0 - 65538.0 * 2.0 ** (-24))
MESH = pl.DeviceIdType.MESH
PHASE_TWO, TWIN = 8, 10
LAST = (((1,), (1,)), ((), ()))
PLAIN = (((1,), (0,)), ((), ()))


def full_dot(a, b, dims):
    return lax.dot_general(
        a, b, dims, precision=lax.Precision.HIGHEST, preferred_element_type=jnp.float32
    )


def half_dot(a, b, dims):
    return lax.dot_general(a, b, dims, preferred_element_type=jnp.float32)


def halves(x):
    high = x.astype(jnp.bfloat16)
    low = (x - high.astype(jnp.float32)).astype(jnp.bfloat16)
    return high, low


def eliminate(m_ref, out_ref, errands=None):
    count = 16
    lane = lax.broadcasted_iota(jnp.int32, (8, 128), 1)
    sub = lax.broadcasted_iota(jnp.int32, (8, 128), 0)
    blocks = [m_ref[8 * i : 8 * i + 8, :] for i in range(count)]
    for j in range(count):
        if errands and j in errands:
            errands[j]()
        first = 8 * j
        block = blocks[j]
        inside = (lane >= first) & (lane < first + 8)
        a, e = {}, {}
        for q in range(8):
            column = jnp.broadcast_to(block[:, first + q : first + q + 1], (8, 128))
            for p in range(q, 8):
                a[p, q] = jnp.broadcast_to(column[p : p + 1, :], (8, 128))
        eye = (lane - first == sub).astype(jnp.float32)
        placed = jnp.where(inside, eye, block)
        lead = [jnp.broadcast_to(placed[m : m + 1, :], (8, 128)) for m in range(8)]
        inverse = [None] * 8
        for k in range(8):
            inverse[k] = 1.0 / a[k, k]
            for i in range(k + 1, 8):
                factor = a[i, k] * inverse[k]
                for q in range(k + 1, i + 1):
                    a[i, q] = a[i, q] - factor * a[q, k]
                lead[i] = lead[i] - factor * lead[k]
                for q in range(k):
                    e[i, q] = e[i, q] - factor * e[k, q]
                e[i, k] = -factor
        scaled = [inverse[m] * lead[m] for m in range(8)]
        solved = list(scaled)
        for m in range(8):
            for n in range(m + 1, 8):
                solved[m] = solved[m] + e[n, m] * scaled[n]
        rows = lead[0] * lax.rsqrt(a[0, 0])
        for m in range(1, 8):
            rows = jnp.where(sub == m, lead[m] * lax.rsqrt(a[m, m]), rows)
        out_ref[first : first + 8, :] = jnp.where(lane <= sub + first, rows, 0.0)
        for i in range(j + 1, count):
            below = blocks[i]
            total = jnp.where(inside, 0.0, below)
            for m in range(8):
                weight = jnp.broadcast_to(below[:, first + m : first + m + 1], (8, 128))
                total = total - weight * solved[m]
            blocks[i] = total


def gather_kernel(
    diag_hbm, panel_hbm, slab_hbm, row_ref, col_ref, slab_ref,
    diag_all, traces, col_all, row_a, row_b, work, inv,
    local_sem, diag_send, diag_recv, rest_send, rest_recv, col_send, col_recv,
    twin_send, twin_recv, part_send, part_recv, one_send, one_recv, two_send, two_recv,
    relay_send, relay_recv,
):
    w, n = lax.axis_index("wide"), lax.axis_index("narrow")
    y, x = lax.div(w, 4), lax.rem(w, 4)
    z, core = lax.div(n, 2), lax.rem(n, 2)

    def piece_at(col, row):
        dx, dy = lax.rem(col + 4 - lax.rem(n, 4), 4), lax.rem(row + 4 - lax.div(n, 4), 4)
        return 4 * lax.rem(dx + dy + z + 2, 4) + dy

    ahead = 1 + 2 * core
    twin = (w, 2 * z + 1 - core)

    def along_x(step):
        return (4 * y + lax.rem(x + step, 4), n)

    def along_y(step):
        return (4 * lax.rem(y + step, 4) + x, n)

    def along_z(step):
        return (w, 2 * lax.rem(z + step, 4) + core)

    def target(half):
        dy = 2 * core + half
        dx = lax.rem(z + 10 - dy - lax.div(w, 2), 4)
        return (4 * lax.rem(y + dy, 4) + lax.rem(x + dx, 4), w)

    source = (n, lax.div(piece_at(x, y), 2))

    slab_copy = pltpu.make_async_copy(slab_hbm, slab_ref, local_sem.at[0])
    diag_own = pltpu.make_async_copy(
        diag_hbm, diag_all.at[pl.ds(pl.multiple_of(32 * n, 32), 32)], local_sem.at[1])
    panel_own = pltpu.make_async_copy(
        panel_hbm, col_all.at[pl.ds(pl.multiple_of(192 * n, 64), 192)], local_sem.at[2])
    diag_own.start()
    panel_own.start()

    barrier = pltpu.get_barrier_semaphore()

    def signal(device):
        pl.semaphore_signal(barrier, inc=1, device_id=device, device_id_type=MESH)

    for step in range(1, 8):
        signal((w, lax.rem(n + step, 8)))
    for step in range(1, 4):
        signal(along_x(step))
        signal(along_y(step))
    signal(source)

    @pl.when(w < 8)
    def _():
        signal(target(0))
        signal(target(1))

    slab_copy.start()
    @pl.when(w < 8)
    def _():
        pl.semaphore_wait(barrier, 16)

    @pl.when(w >= 8)
    def _():
        pl.semaphore_wait(barrier, 14)

    def remote(src, dst, send, recv, device):
        return pltpu.make_async_remote_copy(
            src, dst, send, recv, device_id=device, device_id_type=MESH)

    def corner_copy(step, origin):
        block = diag_all.at[pl.ds(pl.multiple_of(32 * origin, 32), 32), 0:128]
        return remote(block, block, diag_send.at[step], diag_recv.at[origin],
                      (w, lax.rem(n + step, 8)))

    def trace_copy(step, origin):
        return remote(traces.at[origin], traces.at[origin], diag_send.at[step],
                      diag_recv.at[origin], (w, lax.rem(n + step, 8)))

    def rest_copy(step, origin):
        block = diag_all.at[pl.ds(pl.multiple_of(32 * origin, 32), 32)]
        return remote(block, block, rest_send.at[step], rest_recv.at[origin],
                      (w, lax.rem(n + step, 8)))

    line = (y, x)

    def pieces(side, row, first, count):
        start = 192 * row + 48 * first
        return (row_b if side else row_a).at[pl.ds(pl.multiple_of(start, 48), 48 * count)]

    def part_copy(half, side):
        row = lax.rem(target(half)[0], 4) if side else lax.div(target(half)[0], 4)
        return remote(
            col_all.at[pl.ds(pl.multiple_of(192 * n + 96 * half + 48 * side, 48), 48)],
            pieces(side, row, 0, 1), part_send.at[2 * half + side], part_recv.at[side],
            target(half))

    def one_copy(step, side):
        return remote(
            pieces(side, line[side], 0, 1), pieces(side, line[side], 4 - step, 1),
            one_send.at[side, step], one_recv.at[side, step],
            along_y(step) if side else along_x(step))

    def across(step, side):
        return along_x(step) if side else along_y(step)

    def two_copy(step, side, rest):
        block = pieces(side, line[side], 1, 3) if rest else pieces(side, line[side], 0, 1)
        return remote(block, block, two_send.at[side, rest, step], two_recv.at[side, rest, step],
                      across(step, side))

    def relay_copy(side):
        block = pieces(side, lax.rem(line[side] + 4 - ahead, 4), 0, 1)
        return remote(block, block, relay_send.at[side], relay_recv.at[side], across(ahead, side))

    def wait_two(side, forward):
        @pl.when(core == (0 if forward else 1))
        def _():
            two_copy(1, side, 0).wait_recv()

        @pl.when(core == (1 if forward else 0))
        def _():
            two_copy(3, side, 0).wait_recv()

    def col_copy(step):
        block = col_all.at[pl.ds(pl.multiple_of(192 * n, 64), 192)]
        return remote(block, block, col_send.at[step], col_recv.at[step], along_z(step))

    def twin_copy(step):
        origin = 2 * lax.rem(z + 4 - step, 4) + core
        block = col_all.at[pl.ds(pl.multiple_of(192 * origin, 64), 192)]
        return remote(block, block, twin_send.at[step], twin_recv.at[step], twin)

    panel_own.wait()

    @pl.when(w < 8)
    def _():
        for half in range(2):
            for side in range(2):
                part_copy(half, side).start()

    diag_own.wait()
    row_id = lax.broadcasted_iota(jnp.int32, (32, 256), 0)
    col_id = lax.broadcasted_iota(jnp.int32, (32, 256), 1)
    own = diag_all[pl.ds(pl.multiple_of(32 * n, 32), 32), :]
    own = jnp.where(col_id == row_id + 32 * n, own, 0.0)
    own = own[:, 0:128] + own[:, 128:256]
    traces[n] = jnp.sum(own, axis=0, keepdims=True)

    @pl.when(n < 4)
    def _():
        for step in range(1, 8):
            corner_copy(step, n).start()

    @pl.when(n >= 4)
    def _():
        for step in range(1, 8):
            trace_copy(step, n).start()

    @pl.when(n >= 4)
    def _():
        for step in range(1, 8):
            rest_copy(step, n).start()

    def start_cols():
        for step in (1, 3, 2):
            col_copy(step).start()
        twin_copy(0).start()

    def first_phase():
        for side in range(2):
            part_copy(0, side).wait_recv()
            for step in (1, 3, 2):
                one_copy(step, side).start()
            for step in (1, 3):
                two_copy(step, side, 0).start()

    start_cols()
    first_phase()

    for origin in range(4):
        @pl.when(n != origin)
        def _():
            corner_copy(1, origin).wait_recv()
    for origin in range(4, 8):
        @pl.when(n != origin)
        def _():
            trace_copy(1, origin).wait_recv()

    total = jnp.zeros((8, 128), jnp.float32)
    sub = lax.broadcasted_iota(jnp.int32, (8, 128), 0)
    lane = lax.broadcasted_iota(jnp.int32, (8, 128), 1)
    for i in range(16):
        total = total + jnp.where(lane == sub + 8 * i, diag_all[8 * i : 8 * i + 8, 0:128], 0.0)
    total = jnp.sum(total, axis=0, keepdims=True)
    for i in range(4, 8):
        total = total + traces[i]
    shift = unit_gamma * jnp.sum(total, axis=1, keepdims=True) / 256.0

    def shifted(start):
        for i in range(16):
            block = diag_all[start + 8 * i : start + 8 * i + 8, start : start + 128]
            work[start + 8 * i : start + 8 * i + 8, :] = jnp.where(
                lane == sub + 8 * i, block - shift, block)

    def second_phase():
        for side in range(2):
            for step in range(1, 4):
                one_copy(step, side).wait_recv()
            for step in (1, 3, 2):
                two_copy(step, side, 1).start()
        for side in range(2):
            wait_two(side, True)
            relay_copy(side).start()

    def to_twin():
        for step in range(1, 4):
            col_copy(step).wait_recv()
            twin_copy(step).start()

    shifted(0)
    eliminate(work.at[0:128], inv.at[0:128, 0:128], {PHASE_TWO: second_phase})
    inv[0:128, 128:256] = jnp.zeros((128, 128), jnp.float32)
    for origin in range(4, 8):
        @pl.when(n != origin)
        def _():
            rest_copy(1, origin).wait_recv()
    shifted(128)
    first = inv[0:128, 0:128]
    corner = diag_all[128:256, 0:128]
    below = full_dot(corner, first, LAST)
    beside = full_dot(first, corner, LAST)
    work[128:256, :] = work[128:256, :] - full_dot(below, beside, PLAIN)
    eliminate(work.at[128:256], inv.at[128:256, 128:256], {TWIN: to_twin})
    inv[128:256, 0:128] = -full_dot(
        inv[128:256, 128:256], full_dot(below, first, PLAIN), PLAIN)

    inv_high, inv_low = halves(inv[...])

    def solve(raw):
        high, low = halves(raw)
        return halves(half_dot(high, inv_high, LAST) + half_dot(high, inv_low, LAST)
                      + half_dot(low, inv_high, LAST))

    for step in range(4):
        twin_copy(step).wait_recv()
    for start in (0, 768):
        high, low = solve(col_all[start : start + 768, :])
        col_ref[start : start + 768, 0:256] = high
        col_ref[start : start + 768, 256:512] = low
    for side in range(2):
        wait_two(side, False)
        relay_copy(side).wait_recv()
        for step in range(1, 4):
            two_copy(step, side, 1).wait_recv()
        high, low = solve((row_b if side else row_a)[...])
        for slot in range(16):
            row, other = slot // 4, lax.rem(line[1 - side] + slot % 4, 4)
            place = 96 * (piece_at(row, other) if side else piece_at(other, row)) + 48 * side
            place = pl.ds(pl.multiple_of(place, 48), 48)
            row_ref[place, 0:256] = high[48 * slot : 48 * slot + 48]
            row_ref[place, 256:512] = low[48 * slot : 48 * slot + 48]

    @pl.when(n < 4)
    def _():
        for step in range(1, 8):
            corner_copy(step, n).wait_send()

    @pl.when(n >= 4)
    def _():
        for step in range(1, 8):
            trace_copy(step, n).wait_send()
            rest_copy(step, n).wait_send()

    @pl.when(w < 8)
    def _():
        for half in range(2):
            for side in range(2):
                part_copy(half, side).wait_send()

    for side in range(2):
        for step in range(1, 4):
            one_copy(step, side).wait_send()
            two_copy(step, side, 1).wait_send()
        two_copy(1, side, 0).wait_send()
        two_copy(3, side, 0).wait_send()
        relay_copy(side).wait_send()
    for step in range(1, 4):
        col_copy(step).wait_send()
    for step in range(4):
        twin_copy(step).wait_send()
    slab_copy.wait()


def gather_and_solve(diag_block, panel_below, slab):
    rows = panel_below.shape[0]
    vmem = pl.BlockSpec(memory_space=pltpu.VMEM)
    hbm = pl.BlockSpec(memory_space=pltpu.HBM)
    out = jax.ShapeDtypeStruct((8 * rows, 512), jnp.bfloat16)
    sems = pltpu.SemaphoreType.DMA
    return pl.pallas_call(
        gather_kernel,
        out_shape=(out, out, jax.ShapeDtypeStruct(slab.shape, slab.dtype)),
        in_specs=[hbm, hbm, hbm],
        out_specs=(vmem, vmem, vmem),
        scratch_shapes=[
            pltpu.VMEM((256, 256), jnp.float32),
            pltpu.VMEM((8, 1, 128), jnp.float32),
            pltpu.VMEM((8 * rows, 256), jnp.float32),
            pltpu.VMEM((4 * rows, 256), jnp.float32),
            pltpu.VMEM((4 * rows, 256), jnp.float32),
            pltpu.VMEM((256, 128), jnp.float32),
            pltpu.VMEM((256, 256), jnp.float32),
            sems((3,)), sems((8,)), sems((8,)), sems((8,)), sems((8,)), sems((4,)), sems((4,)),
            sems((4,)), sems((4,)), sems((4,)), sems((2,)), sems((2, 4)), sems((2, 4)),
            sems((2, 2, 4)), sems((2, 2, 4)), sems((2,)), sems((2,)),
        ],
        compiler_params=pltpu.CompilerParams(
            collective_id=0, has_side_effects=True, vmem_limit_bytes=28 << 20),
        name="gather_and_solve",
    )(*(pltpu.with_memory_space_constraint(a, pltpu.HBM) for a in (diag_block, panel_below, slab)))


def update_kernel(row_ref, col_ref, slab_ref, out_hbm, buffer, sem):
    rows, cols = slab_ref.shape
    tall, broad, depth = 768, 512, 3
    tiles = [(i, j) for i in range(0, rows, tall) for j in range(0, cols, broad)]

    def out_copy(t):
        i, j = tiles[t]
        return pltpu.make_async_copy(
            buffer.at[t % depth], out_hbm.at[pl.ds(i, tall), pl.ds(j, broad)], sem.at[t % depth])

    for t, (i, j) in enumerate(tiles):
        if t >= depth:
            out_copy(t - depth).wait()
        high, low = row_ref[i : i + tall, 0:256], row_ref[i : i + tall, 256:512]
        col_high, col_low = col_ref[j : j + broad, 0:256], col_ref[j : j + broad, 256:512]
        product = (half_dot(high, col_high, LAST) + half_dot(high, col_low, LAST)
                   + half_dot(low, col_high, LAST))
        buffer[t % depth] = slab_ref[i : i + tall, j : j + broad] - product
        out_copy(t).start()
    for t in range(len(tiles) - depth, len(tiles)):
        out_copy(t).wait()


def update(row_panel, col_panel, slab):
    vmem = pl.BlockSpec(memory_space=pltpu.VMEM)
    return pl.pallas_call(
        update_kernel,
        out_shape=jax.ShapeDtypeStruct(slab.shape, jnp.float32),
        in_specs=[vmem, vmem, vmem],
        out_specs=pl.BlockSpec(memory_space=pltpu.HBM),
        scratch_shapes=[pltpu.VMEM((3, 768, 512), jnp.float32), pltpu.SemaphoreType.DMA((3,))],
        compiler_params=pltpu.CompilerParams(vmem_limit_bytes=24 << 20),
        name="update",
    )(row_panel, col_panel, slab)


def on_device(diag_block, panel_below, trailing_slab):
    row_panel, col_panel, slab = gather_and_solve(diag_block, panel_below, trailing_slab)
    return update(row_panel, col_panel, slab)


def solution(mesh):
    placed = (P("narrow", None), P(("wide", "narrow"), None), P("narrow", "wide"))
    return jax.shard_map(
        on_device, mesh=mesh, in_specs=placed, out_specs=P("narrow", "wide"), check_vma=False
    )
```

```python
import functools

import jax
import jax.numpy as jnp
from jax import lax
from jax.experimental import pallas as pl
from jax.experimental.pallas import tpu as pltpu
from jax.sharding import PartitionSpec as P

unit_gamma = 65538.0 * 2.0 ** (-24) / (1.0 - 65538.0 * 2.0 ** (-24))
MESH = pl.DeviceIdType.MESH
PHASE_TWO, TWIN = 8, 10
LAST = (((1,), (1,)), ((), ()))
PLAIN = (((1,), (0,)), ((), ()))


def full_dot(a, b, dims):
    return lax.dot_general(
        a, b, dims, precision=lax.Precision.HIGHEST, preferred_element_type=jnp.float32
    )


def half_dot(a, b, dims):
    return lax.dot_general(a, b, dims, preferred_element_type=jnp.float32)


def halves(x):
    high = x.astype(jnp.bfloat16)
    low = (x - high.astype(jnp.float32)).astype(jnp.bfloat16)
    return high, low


def eliminate(m_ref, out_ref, errands=None):
    count = 16
    lane = lax.broadcasted_iota(jnp.int32, (8, 128), 1)
    sub = lax.broadcasted_iota(jnp.int32, (8, 128), 0)
    blocks = [m_ref[8 * i : 8 * i + 8, :] for i in range(count)]
    for j in range(count):
        if errands and j in errands:
            errands[j]()
        first = 8 * j
        block = blocks[j]
        inside = (lane >= first) & (lane < first + 8)
        a, e = {}, {}
        for q in range(8):
            column = jnp.broadcast_to(block[:, first + q : first + q + 1], (8, 128))
            for p in range(q, 8):
                a[p, q] = jnp.broadcast_to(column[p : p + 1, :], (8, 128))
        eye = (lane - first == sub).astype(jnp.float32)
        placed = jnp.where(inside, eye, block)
        lead = [jnp.broadcast_to(placed[m : m + 1, :], (8, 128)) for m in range(8)]
        inverse = [None] * 8
        for k in range(8):
            inverse[k] = 1.0 / a[k, k]
            for i in range(k + 1, 8):
                factor = a[i, k] * inverse[k]
                for q in range(k + 1, i + 1):
                    a[i, q] = a[i, q] - factor * a[q, k]
                lead[i] = lead[i] - factor * lead[k]
                for q in range(k):
                    e[i, q] = e[i, q] - factor * e[k, q]
                e[i, k] = -factor
        scaled = [inverse[m] * lead[m] for m in range(8)]
        solved = list(scaled)
        for m in range(8):
            for n in range(m + 1, 8):
                solved[m] = solved[m] + e[n, m] * scaled[n]
        rows = lead[0] * lax.rsqrt(a[0, 0])
        for m in range(1, 8):
            rows = jnp.where(sub == m, lead[m] * lax.rsqrt(a[m, m]), rows)
        out_ref[first : first + 8, :] = jnp.where(lane <= sub + first, rows, 0.0)
        for i in range(j + 1, count):
            below = blocks[i]
            total = jnp.where(inside, 0.0, below)
            for m in range(8):
                weight = jnp.broadcast_to(below[:, first + m : first + m + 1], (8, 128))
                total = total - weight * solved[m]
            blocks[i] = total


def gather_kernel(
    diag_hbm, panel_hbm, slab_hbm, row_ref, col_ref, slab_ref,
    diag_all, traces, col_all, row_a, row_b, work, inv,
    local_sem, diag_send, diag_recv, rest_send, rest_recv, col_send, col_recv,
    twin_send, twin_recv, part_send, part_recv, one_send, one_recv, two_send, two_recv,
    relay_send, relay_recv,
):
    w, n = lax.axis_index("wide"), lax.axis_index("narrow")
    y, x = lax.div(w, 4), lax.rem(w, 4)
    z, core = lax.div(n, 2), lax.rem(n, 2)

    def piece_at(col, row):
        dx, dy = lax.rem(col + 4 - lax.rem(n, 4), 4), lax.rem(row + 4 - lax.div(n, 4), 4)
        return 4 * lax.rem(dx + dy + z + 2, 4) + dy

    ahead = 1 + 2 * core
    twin = (w, 2 * z + 1 - core)

    def along_x(step):
        return (4 * y + lax.rem(x + step, 4), n)

    def along_y(step):
        return (4 * lax.rem(y + step, 4) + x, n)

    def along_z(step):
        return (w, 2 * lax.rem(z + step, 4) + core)

    def target(half):
        dy = 2 * core + half
        dx = lax.rem(z + 10 - dy - lax.div(w, 2), 4)
        return (4 * lax.rem(y + dy, 4) + lax.rem(x + dx, 4), w)

    source = (n, lax.div(piece_at(x, y), 2))

    slab_copy = pltpu.make_async_copy(slab_hbm, slab_ref, local_sem.at[0])
    diag_own = pltpu.make_async_copy(
        diag_hbm, diag_all.at[pl.ds(pl.multiple_of(32 * n, 32), 32)], local_sem.at[1])
    panel_own = pltpu.make_async_copy(
        panel_hbm, col_all.at[pl.ds(pl.multiple_of(192 * n, 64), 192)], local_sem.at[2])
    diag_own.start()
    panel_own.start()

    barrier = pltpu.get_barrier_semaphore()

    def signal(device):
        pl.semaphore_signal(barrier, inc=1, device_id=device, device_id_type=MESH)

    for step in range(1, 8):
        signal((w, lax.rem(n + step, 8)))
    for step in range(1, 4):
        signal(along_x(step))
        signal(along_y(step))
    signal(source)

    @pl.when(w < 8)
    def _():
        signal(target(0))
        signal(target(1))

    slab_copy.start()
    @pl.when(w < 8)
    def _():
        pl.semaphore_wait(barrier, 16)

    @pl.when(w >= 8)
    def _():
        pl.semaphore_wait(barrier, 14)

    def remote(src, dst, send, recv, device):
        return pltpu.make_async_remote_copy(
            src, dst, send, recv, device_id=device, device_id_type=MESH)

    def corner_copy(step, origin):
        block = diag_all.at[pl.ds(pl.multiple_of(32 * origin, 32), 32), 0:128]
        return remote(block, block, diag_send.at[step], diag_recv.at[origin],
                      (w, lax.rem(n + step, 8)))

    def trace_copy(step, origin):
        return remote(traces.at[origin], traces.at[origin], diag_send.at[step],
                      diag_recv.at[origin], (w, lax.rem(n + step, 8)))

    def rest_copy(step, origin):
        block = diag_all.at[pl.ds(pl.multiple_of(32 * origin, 32), 32)]
        return remote(block, block, rest_send.at[step], rest_recv.at[origin],
                      (w, lax.rem(n + step, 8)))

    line = (y, x)

    def pieces(side, row, first, count):
        start = 192 * row + 48 * first
        return (row_b if side else row_a).at[pl.ds(pl.multiple_of(start, 48), 48 * count)]

    def part_copy(half, side):
        row = lax.rem(target(half)[0], 4) if side else lax.div(target(half)[0], 4)
        return remote(
            col_all.at[pl.ds(pl.multiple_of(192 * n + 96 * half + 48 * side, 48), 48)],
            pieces(side, row, 0, 1), part_send.at[2 * half + side], part_recv.at[side],
            target(half))

    def one_copy(step, side):
        return remote(
            pieces(side, line[side], 0, 1), pieces(side, line[side], 4 - step, 1),
            one_send.at[side, step], one_recv.at[side, step],
            along_y(step) if side else along_x(step))

    def across(step, side):
        return along_x(step) if side else along_y(step)

    def two_copy(step, side, rest):
        block = pieces(side, line[side], 1, 3) if rest else pieces(side, line[side], 0, 1)
        return remote(block, block, two_send.at[side, rest, step], two_recv.at[side, rest, step],
                      across(step, side))

    def relay_copy(side):
        block = pieces(side, lax.rem(line[side] + 4 - ahead, 4), 0, 1)
        return remote(block, block, relay_send.at[side], relay_recv.at[side], across(ahead, side))

    def wait_two(side, forward):
        @pl.when(core == (0 if forward else 1))
        def _():
            two_copy(1, side, 0).wait_recv()

        @pl.when(core == (1 if forward else 0))
        def _():
            two_copy(3, side, 0).wait_recv()

    def col_copy(step):
        block = col_all.at[pl.ds(pl.multiple_of(192 * n, 64), 192)]
        return remote(block, block, col_send.at[step], col_recv.at[step], along_z(step))

    def twin_copy(step):
        origin = 2 * lax.rem(z + 4 - step, 4) + core
        block = col_all.at[pl.ds(pl.multiple_of(192 * origin, 64), 192)]
        return remote(block, block, twin_send.at[step], twin_recv.at[step], twin)

    panel_own.wait()

    @pl.when(w < 8)
    def _():
        for half in range(2):
            for side in range(2):
                part_copy(half, side).start()

    diag_own.wait()
    row_id = lax.broadcasted_iota(jnp.int32, (32, 256), 0)
    col_id = lax.broadcasted_iota(jnp.int32, (32, 256), 1)
    own = diag_all[pl.ds(pl.multiple_of(32 * n, 32), 32), :]
    own = jnp.where(col_id == row_id + 32 * n, own, 0.0)
    own = own[:, 0:128] + own[:, 128:256]
    traces[n] = jnp.sum(own, axis=0, keepdims=True)

    @pl.when(n < 4)
    def _():
        for step in range(1, 8):
            corner_copy(step, n).start()

    @pl.when(n >= 4)
    def _():
        for step in range(1, 8):
            trace_copy(step, n).start()

    @pl.when(n >= 4)
    def _():
        for step in range(1, 8):
            rest_copy(step, n).start()

    def start_cols():
        for step in (1, 3, 2):
            col_copy(step).start()
        twin_copy(0).start()

    def first_phase():
        for side in range(2):
            part_copy(0, side).wait_recv()
            for step in (1, 3, 2):
                one_copy(step, side).start()
            for step in (1, 3):
                two_copy(step, side, 0).start()

    start_cols()
    first_phase()

    for origin in range(4):
        @pl.when(n != origin)
        def _():
            corner_copy(1, origin).wait_recv()
    for origin in range(4, 8):
        @pl.when(n != origin)
        def _():
            trace_copy(1, origin).wait_recv()

    total = jnp.zeros((8, 128), jnp.float32)
    sub = lax.broadcasted_iota(jnp.int32, (8, 128), 0)
    lane = lax.broadcasted_iota(jnp.int32, (8, 128), 1)
    for i in range(16):
        total = total + jnp.where(lane == sub + 8 * i, diag_all[8 * i : 8 * i + 8, 0:128], 0.0)
    total = jnp.sum(total, axis=0, keepdims=True)
    for i in range(4, 8):
        total = total + traces[i]
    shift = unit_gamma * jnp.sum(total, axis=1, keepdims=True) / 256.0

    def shifted(start):
        for i in range(16):
            block = diag_all[start + 8 * i : start + 8 * i + 8, start : start + 128]
            work[start + 8 * i : start + 8 * i + 8, :] = jnp.where(
                lane == sub + 8 * i, block - shift, block)

    def second_phase():
        for side in range(2):
            for step in range(1, 4):
                one_copy(step, side).wait_recv()
            for step in (1, 3, 2):
                two_copy(step, side, 1).start()
        for side in range(2):
            wait_two(side, True)
            relay_copy(side).start()

    def to_twin():
        for step in range(1, 4):
            col_copy(step).wait_recv()
            twin_copy(step).start()

    shifted(0)
    eliminate(work.at[0:128], inv.at[0:128, 0:128], {PHASE_TWO: second_phase})
    inv[0:128, 128:256] = jnp.zeros((128, 128), jnp.float32)
    for origin in range(4, 8):
        @pl.when(n != origin)
        def _():
            rest_copy(1, origin).wait_recv()
    shifted(128)
    first = inv[0:128, 0:128]
    corner = diag_all[128:256, 0:128]
    below = full_dot(corner, first, LAST)
    beside = full_dot(first, corner, LAST)
    work[128:256, :] = work[128:256, :] - full_dot(below, beside, PLAIN)
    eliminate(work.at[128:256], inv.at[128:256, 128:256], {TWIN: to_twin})
    inv[128:256, 0:128] = -full_dot(
        inv[128:256, 128:256], full_dot(below, first, PLAIN), PLAIN)

    inv_high, inv_low = halves(inv[...])

    def solve(raw):
        high, low = halves(raw)
        return halves(half_dot(high, inv_high, LAST) + half_dot(high, inv_low, LAST)
                      + half_dot(low, inv_high, LAST))

    for step in range(4):
        twin_copy(step).wait_recv()
    for start in (0, 768):
        high, low = solve(col_all[start : start + 768, :])
        col_ref[start : start + 768, 0:256] = high
        col_ref[start : start + 768, 256:512] = low
    for side in range(2):
        wait_two(side, False)
        relay_copy(side).wait_recv()
        for step in range(1, 4):
            two_copy(step, side, 1).wait_recv()
        high, low = solve((row_b if side else row_a)[...])
        for slot in range(16):
            row, other = slot // 4, lax.rem(line[1 - side] + slot % 4, 4)
            place = 96 * (piece_at(row, other) if side else piece_at(other, row)) + 48 * side
            place = pl.ds(pl.multiple_of(place, 48), 48)
            row_ref[place, 0:256] = high[48 * slot : 48 * slot + 48]
            row_ref[place, 256:512] = low[48 * slot : 48 * slot + 48]

    @pl.when(n < 4)
    def _():
        for step in range(1, 8):
            corner_copy(step, n).wait_send()

    @pl.when(n >= 4)
    def _():
        for step in range(1, 8):
            trace_copy(step, n).wait_send()
            rest_copy(step, n).wait_send()

    @pl.when(w < 8)
    def _():
        for half in range(2):
            for side in range(2):
                part_copy(half, side).wait_send()

    for side in range(2):
        for step in range(1, 4):
            one_copy(step, side).wait_send()
            two_copy(step, side, 1).wait_send()
        two_copy(1, side, 0).wait_send()
        two_copy(3, side, 0).wait_send()
        relay_copy(side).wait_send()
    for step in range(1, 4):
        col_copy(step).wait_send()
    for step in range(4):
        twin_copy(step).wait_send()
    slab_copy.wait()


def gather_and_solve(diag_block, panel_below, slab):
    rows = panel_below.shape[0]
    vmem = pl.BlockSpec(memory_space=pltpu.VMEM)
    hbm = pl.BlockSpec(memory_space=pltpu.HBM)
    out = jax.ShapeDtypeStruct((8 * rows, 512), jnp.bfloat16)
    sems = pltpu.SemaphoreType.DMA
    return pl.pallas_call(
        gather_kernel,
        out_shape=(out, out, jax.ShapeDtypeStruct(slab.shape, slab.dtype)),
        in_specs=[hbm, hbm, hbm],
        out_specs=(vmem, vmem, vmem),
        scratch_shapes=[
            pltpu.VMEM((256, 256), jnp.float32),
            pltpu.VMEM((8, 1, 128), jnp.float32),
            pltpu.VMEM((8 * rows, 256), jnp.float32),
            pltpu.VMEM((4 * rows, 256), jnp.float32),
            pltpu.VMEM((4 * rows, 256), jnp.float32),
            pltpu.VMEM((256, 128), jnp.float32),
            pltpu.VMEM((256, 256), jnp.float32),
            sems((3,)), sems((8,)), sems((8,)), sems((8,)), sems((8,)), sems((4,)), sems((4,)),
            sems((4,)), sems((4,)), sems((4,)), sems((2,)), sems((2, 4)), sems((2, 4)),
            sems((2, 2, 4)), sems((2, 2, 4)), sems((2,)), sems((2,)),
        ],
        compiler_params=pltpu.CompilerParams(
            collective_id=0, has_side_effects=True, vmem_limit_bytes=28 << 20),
        name="gather_and_solve",
    )(*(pltpu.with_memory_space_constraint(a, pltpu.HBM) for a in (diag_block, panel_below, slab)))


def update_kernel(row_ref, col_ref, slab_ref, out_hbm, buffer, sem):
    rows, cols = slab_ref.shape
    tall, broad = 384, 512
    copies = []
    for i in range(0, rows, tall):
        for j in range(0, cols, broad):
            t = len(copies)
            high, low = row_ref[i : i + tall, 0:256], row_ref[i : i + tall, 256:512]
            col_high, col_low = col_ref[j : j + broad, 0:256], col_ref[j : j + broad, 256:512]
            product = (half_dot(high, col_high, LAST) + half_dot(high, col_low, LAST)
                       + half_dot(low, col_high, LAST))
            buffer[i : i + tall, j : j + broad] = slab_ref[i : i + tall, j : j + broad] - product
            copies.append(pltpu.make_async_copy(
                buffer.at[pl.ds(i, tall), pl.ds(j, broad)],
                out_hbm.at[pl.ds(i, tall), pl.ds(j, broad)], sem.at[t]))
            copies[-1].start()
    for copy in copies:
        copy.wait()


def update(row_panel, col_panel, slab):
    vmem = pl.BlockSpec(memory_space=pltpu.VMEM)
    return pl.pallas_call(
        update_kernel,
        out_shape=jax.ShapeDtypeStruct(slab.shape, jnp.float32),
        in_specs=[vmem, vmem, vmem],
        out_specs=pl.BlockSpec(memory_space=pltpu.HBM),
        scratch_shapes=[pltpu.VMEM(slab.shape, jnp.float32), pltpu.SemaphoreType.DMA((12,))],
        compiler_params=pltpu.CompilerParams(vmem_limit_bytes=24 << 20),
        name="update",
    )(row_panel, col_panel, slab)


def on_device(diag_block, panel_below, trailing_slab):
    row_panel, col_panel, slab = gather_and_solve(diag_block, panel_below, trailing_slab)
    return update(row_panel, col_panel, slab)


def solution(mesh):
    placed = (P("narrow", None), P(("wide", "narrow"), None), P("narrow", "wide"))
    return jax.shard_map(
        on_device, mesh=mesh, in_specs=placed, out_specs=P("narrow", "wide"), check_vma=False
    )
```

```python
import functools

import jax
import jax.numpy as jnp
from jax import lax
from jax.experimental import pallas as pl
from jax.experimental.pallas import tpu as pltpu
from jax.sharding import PartitionSpec as P

unit_gamma = 65538.0 * 2.0 ** (-24) / (1.0 - 65538.0 * 2.0 ** (-24))
MESH = pl.DeviceIdType.MESH
PHASE_TWO, TWIN = 10, 10
LAST = (((1,), (1,)), ((), ()))
PLAIN = (((1,), (0,)), ((), ()))


def full_dot(a, b, dims):
    return lax.dot_general(
        a, b, dims, precision=lax.Precision.HIGHEST, preferred_element_type=jnp.float32
    )


def half_dot(a, b, dims):
    return lax.dot_general(a, b, dims, preferred_element_type=jnp.float32)


def halves(x):
    high = x.astype(jnp.bfloat16)
    low = (x - high.astype(jnp.float32)).astype(jnp.bfloat16)
    return high, low


def eliminate(m_ref, out_ref, errands=None):
    count = 16
    lane = lax.broadcasted_iota(jnp.int32, (8, 128), 1)
    sub = lax.broadcasted_iota(jnp.int32, (8, 128), 0)
    blocks = [m_ref[8 * i : 8 * i + 8, :] for i in range(count)]
    for j in range(count):
        if errands and j in errands:
            errands[j]()
        first = 8 * j
        block = blocks[j]
        inside = (lane >= first) & (lane < first + 8)
        a, e = {}, {}
        for q in range(8):
            column = jnp.broadcast_to(block[:, first + q : first + q + 1], (8, 128))
            for p in range(q, 8):
                a[p, q] = jnp.broadcast_to(column[p : p + 1, :], (8, 128))
        eye = (lane - first == sub).astype(jnp.float32)
        placed = jnp.where(inside, eye, block)
        lead = [jnp.broadcast_to(placed[m : m + 1, :], (8, 128)) for m in range(8)]
        inverse = [None] * 8
        for k in range(8):
            inverse[k] = 1.0 / a[k, k]
            for i in range(k + 1, 8):
                factor = a[i, k] * inverse[k]
                for q in range(k + 1, i + 1):
                    a[i, q] = a[i, q] - factor * a[q, k]
                lead[i] = lead[i] - factor * lead[k]
                for q in range(k):
                    e[i, q] = e[i, q] - factor * e[k, q]
                e[i, k] = -factor
        scaled = [inverse[m] * lead[m] for m in range(8)]
        solved = list(scaled)
        for m in range(8):
            for n in range(m + 1, 8):
                solved[m] = solved[m] + e[n, m] * scaled[n]
        rows = lead[0] * lax.rsqrt(a[0, 0])
        for m in range(1, 8):
            rows = jnp.where(sub == m, lead[m] * lax.rsqrt(a[m, m]), rows)
        out_ref[first : first + 8, :] = jnp.where(lane <= sub + first, rows, 0.0)
        for i in range(j + 1, count):
            below = blocks[i]
            total = jnp.where(inside, 0.0, below)
            for m in range(8):
                weight = jnp.broadcast_to(below[:, first + m : first + m + 1], (8, 128))
                total = total - weight * solved[m]
            blocks[i] = total


def gather_kernel(
    diag_hbm, panel_hbm, slab_hbm, row_ref, col_ref, slab_ref,
    diag_all, traces, col_all, row_a, row_b, work, inv,
    local_sem, diag_send, diag_recv, rest_send, rest_recv, col_send, col_recv,
    twin_send, twin_recv, part_send, part_recv, one_send, one_recv, two_send, two_recv,
    relay_send, relay_recv,
):
    w, n = lax.axis_index("wide"), lax.axis_index("narrow")
    y, x = lax.div(w, 4), lax.rem(w, 4)
    z, core = lax.div(n, 2), lax.rem(n, 2)

    def piece_at(col, row):
        dx, dy = lax.rem(col + 4 - lax.rem(n, 4), 4), lax.rem(row + 4 - lax.div(n, 4), 4)
        return 4 * lax.rem(dx + dy + z + 2, 4) + dy

    ahead = 1 + 2 * core
    twin = (w, 2 * z + 1 - core)

    def along_x(step):
        return (4 * y + lax.rem(x + step, 4), n)

    def along_y(step):
        return (4 * lax.rem(y + step, 4) + x, n)

    def along_z(step):
        return (w, 2 * lax.rem(z + step, 4) + core)

    def target(half):
        dy = 2 * core + half
        dx = lax.rem(z + 10 - dy - lax.div(w, 2), 4)
        return (4 * lax.rem(y + dy, 4) + lax.rem(x + dx, 4), w)

    source = (n, lax.div(piece_at(x, y), 2))

    slab_copy = pltpu.make_async_copy(slab_hbm, slab_ref, local_sem.at[0])
    diag_own = pltpu.make_async_copy(
        diag_hbm, diag_all.at[pl.ds(pl.multiple_of(32 * n, 32), 32)], local_sem.at[1])
    panel_own = pltpu.make_async_copy(
        panel_hbm, col_all.at[pl.ds(pl.multiple_of(192 * n, 64), 192)], local_sem.at[2])
    diag_own.start()
    panel_own.start()

    barrier = pltpu.get_barrier_semaphore()

    def signal(device):
        pl.semaphore_signal(barrier, inc=1, device_id=device, device_id_type=MESH)

    for step in range(1, 8):
        signal((w, lax.rem(n + step, 8)))
    for step in range(1, 4):
        signal(along_x(step))
        signal(along_y(step))
    signal(source)

    @pl.when(w < 8)
    def _():
        signal(target(0))
        signal(target(1))

    slab_copy.start()
    @pl.when(w < 8)
    def _():
        pl.semaphore_wait(barrier, 16)

    @pl.when(w >= 8)
    def _():
        pl.semaphore_wait(barrier, 14)

    def remote(src, dst, send, recv, device):
        return pltpu.make_async_remote_copy(
            src, dst, send, recv, device_id=device, device_id_type=MESH)

    def corner_copy(step, origin):
        block = diag_all.at[pl.ds(pl.multiple_of(32 * origin, 32), 32), 0:128]
        return remote(block, block, diag_send.at[step], diag_recv.at[origin],
                      (w, lax.rem(n + step, 8)))

    def trace_copy(step, origin):
        return remote(traces.at[origin], traces.at[origin], diag_send.at[step],
                      diag_recv.at[origin], (w, lax.rem(n + step, 8)))

    def rest_copy(step, origin):
        block = diag_all.at[pl.ds(pl.multiple_of(32 * origin, 32), 32)]
        return remote(block, block, rest_send.at[step], rest_recv.at[origin],
                      (w, lax.rem(n + step, 8)))

    line = (y, x)

    def pieces(side, row, first, count):
        start = 192 * row + 48 * first
        return (row_b if side else row_a).at[pl.ds(pl.multiple_of(start, 48), 48 * count)]

    def part_copy(half, side):
        row = lax.rem(target(half)[0], 4) if side else lax.div(target(half)[0], 4)
        return remote(
            col_all.at[pl.ds(pl.multiple_of(192 * n + 96 * half + 48 * side, 48), 48)],
            pieces(side, row, 0, 1), part_send.at[2 * half + side], part_recv.at[side],
            target(half))

    def one_copy(step, side):
        return remote(
            pieces(side, line[side], 0, 1), pieces(side, line[side], 4 - step, 1),
            one_send.at[side, step], one_recv.at[side, step],
            along_y(step) if side else along_x(step))

    def across(step, side):
        return along_x(step) if side else along_y(step)

    def two_copy(step, side, rest):
        block = pieces(side, line[side], 1, 3) if rest else pieces(side, line[side], 0, 1)
        return remote(block, block, two_send.at[side, rest, step], two_recv.at[side, rest, step],
                      across(step, side))

    def relay_copy(side):
        block = pieces(side, lax.rem(line[side] + 4 - ahead, 4), 0, 1)
        return remote(block, block, relay_send.at[side], relay_recv.at[side], across(ahead, side))

    def wait_two(side, forward):
        @pl.when(core == (0 if forward else 1))
        def _():
            two_copy(1, side, 0).wait_recv()

        @pl.when(core == (1 if forward else 0))
        def _():
            two_copy(3, side, 0).wait_recv()

    def col_copy(step):
        block = col_all.at[pl.ds(pl.multiple_of(192 * n, 64), 192)]
        return remote(block, block, col_send.at[step], col_recv.at[step], along_z(step))

    def twin_copy(step):
        origin = 2 * lax.rem(z + 4 - step, 4) + core
        block = col_all.at[pl.ds(pl.multiple_of(192 * origin, 64), 192)]
        return remote(block, block, twin_send.at[step], twin_recv.at[step], twin)

    panel_own.wait()

    @pl.when(w < 8)
    def _():
        for half in range(2):
            for side in range(2):
                part_copy(half, side).start()

    diag_own.wait()
    row_id = lax.broadcasted_iota(jnp.int32, (32, 256), 0)
    col_id = lax.broadcasted_iota(jnp.int32, (32, 256), 1)
    own = diag_all[pl.ds(pl.multiple_of(32 * n, 32), 32), :]
    own = jnp.where(col_id == row_id + 32 * n, own, 0.0)
    own = own[:, 0:128] + own[:, 128:256]
    traces[n] = jnp.sum(own, axis=0, keepdims=True)

    @pl.when(n < 4)
    def _():
        for step in range(1, 8):
            corner_copy(step, n).start()

    @pl.when(n >= 4)
    def _():
        for step in range(1, 8):
            trace_copy(step, n).start()

    @pl.when(n >= 4)
    def _():
        for step in range(1, 8):
            rest_copy(step, n).start()

    def start_cols():
        for step in (1, 3, 2):
            col_copy(step).start()
        twin_copy(0).start()

    def first_phase():
        for side in range(2):
            part_copy(0, side).wait_recv()
            for step in (1, 3, 2):
                one_copy(step, side).start()
            for step in (1, 3):
                two_copy(step, side, 0).start()

    start_cols()
    first_phase()

    for origin in range(4):
        @pl.when(n != origin)
        def _():
            corner_copy(1, origin).wait_recv()
    for origin in range(4, 8):
        @pl.when(n != origin)
        def _():
            trace_copy(1, origin).wait_recv()

    total = jnp.zeros((8, 128), jnp.float32)
    sub = lax.broadcasted_iota(jnp.int32, (8, 128), 0)
    lane = lax.broadcasted_iota(jnp.int32, (8, 128), 1)
    for i in range(16):
        total = total + jnp.where(lane == sub + 8 * i, diag_all[8 * i : 8 * i + 8, 0:128], 0.0)
    total = jnp.sum(total, axis=0, keepdims=True)
    for i in range(4, 8):
        total = total + traces[i]
    shift = unit_gamma * jnp.sum(total, axis=1, keepdims=True) / 256.0

    def shifted(start):
        for i in range(16):
            block = diag_all[start + 8 * i : start + 8 * i + 8, start : start + 128]
            work[start + 8 * i : start + 8 * i + 8, :] = jnp.where(
                lane == sub + 8 * i, block - shift, block)

    def second_phase():
        for side in range(2):
            for step in range(1, 4):
                one_copy(step, side).wait_recv()
            for step in (1, 3, 2):
                two_copy(step, side, 1).start()
        for side in range(2):
            wait_two(side, True)
            relay_copy(side).start()

    def to_twin():
        for step in range(1, 4):
            col_copy(step).wait_recv()
            twin_copy(step).start()

    shifted(0)
    eliminate(work.at[0:128], inv.at[0:128, 0:128], {PHASE_TWO: second_phase})
    inv[0:128, 128:256] = jnp.zeros((128, 128), jnp.float32)
    for origin in range(4, 8):
        @pl.when(n != origin)
        def _():
            rest_copy(1, origin).wait_recv()
    shifted(128)
    first = inv[0:128, 0:128]
    corner = diag_all[128:256, 0:128]
    below = full_dot(corner, first, LAST)
    beside = full_dot(first, corner, LAST)
    work[128:256, :] = work[128:256, :] - full_dot(below, beside, PLAIN)
    eliminate(work.at[128:256], inv.at[128:256, 128:256], {TWIN: to_twin})
    inv[128:256, 0:128] = -full_dot(
        inv[128:256, 128:256], full_dot(below, first, PLAIN), PLAIN)

    inv_high, inv_low = halves(inv[...])

    def solve(raw):
        high, low = halves(raw)
        return halves(half_dot(high, inv_high, LAST) + half_dot(high, inv_low, LAST)
                      + half_dot(low, inv_high, LAST))

    for step in range(4):
        twin_copy(step).wait_recv()
    for start in (0, 768):
        high, low = solve(col_all[start : start + 768, :])
        col_ref[start : start + 768, 0:256] = high
        col_ref[start : start + 768, 256:512] = low
    def place_rows(side, slots, halved):
        for k, (row, step) in enumerate(slots):
            row, other = lax.rem(line[side] + row, 4), lax.rem(line[1 - side] + step, 4)
            place = 96 * (piece_at(row, other) if side else piece_at(other, row)) + 48 * side
            place = pl.ds(pl.multiple_of(place, 48), 48)
            row_ref[place, 0:256] = halved[0][48 * k : 48 * k + 48]
            row_ref[place, 256:512] = halved[1][48 * k : 48 * k + 48]

    early = solve(jnp.concatenate([pieces(side, line[side], 0, 4)[...] for side in range(2)], axis=0))
    for side in range(2):
        rows = slice(192 * side, 192 * side + 192)
        place_rows(side, [(0, j) for j in range(4)], (early[0][rows], early[1][rows]))

    for side in range(2):
        wait_two(side, False)
        relay_copy(side).wait_recv()
        for step in range(1, 4):
            two_copy(step, side, 1).wait_recv()
        late = [pieces(side, lax.rem(line[side] + i, 4), 0, 4)[...] for i in range(1, 4)]
        place_rows(side, [(i, j) for i in range(1, 4) for j in range(4)],
                   solve(jnp.concatenate(late, axis=0)))

    @pl.when(n < 4)
    def _():
        for step in range(1, 8):
            corner_copy(step, n).wait_send()

    @pl.when(n >= 4)
    def _():
        for step in range(1, 8):
            trace_copy(step, n).wait_send()
            rest_copy(step, n).wait_send()

    @pl.when(w < 8)
    def _():
        for half in range(2):
            for side in range(2):
                part_copy(half, side).wait_send()

    for side in range(2):
        for step in range(1, 4):
            one_copy(step, side).wait_send()
            two_copy(step, side, 1).wait_send()
        two_copy(1, side, 0).wait_send()
        two_copy(3, side, 0).wait_send()
        relay_copy(side).wait_send()
    for step in range(1, 4):
        col_copy(step).wait_send()
    for step in range(4):
        twin_copy(step).wait_send()
    slab_copy.wait()


def gather_and_solve(diag_block, panel_below, slab):
    rows = panel_below.shape[0]
    vmem = pl.BlockSpec(memory_space=pltpu.VMEM)
    hbm = pl.BlockSpec(memory_space=pltpu.HBM)
    out = jax.ShapeDtypeStruct((8 * rows, 512), jnp.bfloat16)
    sems = pltpu.SemaphoreType.DMA
    return pl.pallas_call(
        gather_kernel,
        out_shape=(out, out, jax.ShapeDtypeStruct(slab.shape, slab.dtype)),
        in_specs=[hbm, hbm, hbm],
        out_specs=(vmem, vmem, vmem),
        scratch_shapes=[
            pltpu.VMEM((256, 256), jnp.float32),
            pltpu.VMEM((8, 1, 128), jnp.float32),
            pltpu.VMEM((8 * rows, 256), jnp.float32),
            pltpu.VMEM((4 * rows, 256), jnp.float32),
            pltpu.VMEM((4 * rows, 256), jnp.float32),
            pltpu.VMEM((256, 128), jnp.float32),
            pltpu.VMEM((256, 256), jnp.float32),
            sems((3,)), sems((8,)), sems((8,)), sems((8,)), sems((8,)), sems((4,)), sems((4,)),
            sems((4,)), sems((4,)), sems((4,)), sems((2,)), sems((2, 4)), sems((2, 4)),
            sems((2, 2, 4)), sems((2, 2, 4)), sems((2,)), sems((2,)),
        ],
        compiler_params=pltpu.CompilerParams(
            collective_id=0, has_side_effects=True, vmem_limit_bytes=28 << 20),
        name="gather_and_solve",
    )(*(pltpu.with_memory_space_constraint(a, pltpu.HBM) for a in (diag_block, panel_below, slab)))


def update_kernel(row_ref, col_ref, slab_ref, out_hbm, buffer, sem):
    rows, cols = slab_ref.shape
    tall, broad = 384, 512
    copies = []
    for i in range(0, rows, tall):
        for j in range(0, cols, broad):
            t = len(copies)
            high, low = row_ref[i : i + tall, 0:256], row_ref[i : i + tall, 256:512]
            col_high, col_low = col_ref[j : j + broad, 0:256], col_ref[j : j + broad, 256:512]
            product = (half_dot(high, col_high, LAST) + half_dot(high, col_low, LAST)
                       + half_dot(low, col_high, LAST))
            buffer[i : i + tall, j : j + broad] = slab_ref[i : i + tall, j : j + broad] - product
            copies.append(pltpu.make_async_copy(
                buffer.at[pl.ds(i, tall), pl.ds(j, broad)],
                out_hbm.at[pl.ds(i, tall), pl.ds(j, broad)], sem.at[t]))
            copies[-1].start()
    for copy in copies:
        copy.wait()


def update(row_panel, col_panel, slab):
    vmem = pl.BlockSpec(memory_space=pltpu.VMEM)
    return pl.pallas_call(
        update_kernel,
        out_shape=jax.ShapeDtypeStruct(slab.shape, jnp.float32),
        in_specs=[vmem, vmem, vmem],
        out_specs=pl.BlockSpec(memory_space=pltpu.HBM),
        scratch_shapes=[pltpu.VMEM(slab.shape, jnp.float32), pltpu.SemaphoreType.DMA((12,))],
        compiler_params=pltpu.CompilerParams(vmem_limit_bytes=24 << 20),
        name="update",
    )(row_panel, col_panel, slab)


def on_device(diag_block, panel_below, trailing_slab):
    row_panel, col_panel, slab = gather_and_solve(diag_block, panel_below, trailing_slab)
    return update(row_panel, col_panel, slab)


def solution(mesh):
    placed = (P("narrow", None), P(("wide", "narrow"), None), P("narrow", "wide"))
    return jax.shard_map(
        on_device, mesh=mesh, in_specs=placed, out_specs=P("narrow", "wide"), check_vma=False
    )
```

```python
import functools

import jax
import jax.numpy as jnp
from jax import lax
from jax.experimental import pallas as pl
from jax.experimental.pallas import tpu as pltpu
from jax.sharding import PartitionSpec as P

unit_gamma = 65538.0 * 2.0 ** (-24) / (1.0 - 65538.0 * 2.0 ** (-24))
MESH = pl.DeviceIdType.MESH
PHASE_TWO, TWIN = 10, 10
LAST = (((1,), (1,)), ((), ()))
PLAIN = (((1,), (0,)), ((), ()))


def full_dot(a, b, dims):
    return lax.dot_general(
        a, b, dims, precision=lax.Precision.HIGHEST, preferred_element_type=jnp.float32
    )


def half_dot(a, b, dims):
    return lax.dot_general(a, b, dims, preferred_element_type=jnp.float32)


def halves(x):
    high = x.astype(jnp.bfloat16)
    low = (x - high.astype(jnp.float32)).astype(jnp.bfloat16)
    return high, low


def eliminate(m_ref, out_ref, errands=None):
    count = 16
    lane = lax.broadcasted_iota(jnp.int32, (8, 128), 1)
    sub = lax.broadcasted_iota(jnp.int32, (8, 128), 0)
    blocks = [m_ref[8 * i : 8 * i + 8, :] for i in range(count)]
    for j in range(count):
        if errands and j in errands:
            errands[j]()
        first = 8 * j
        block = blocks[j]
        inside = (lane >= first) & (lane < first + 8)
        a, e = {}, {}
        for q in range(8):
            column = jnp.broadcast_to(block[:, first + q : first + q + 1], (8, 128))
            for p in range(q, 8):
                a[p, q] = jnp.broadcast_to(column[p : p + 1, :], (8, 128))
        eye = (lane - first == sub).astype(jnp.float32)
        placed = jnp.where(inside, eye, block)
        lead = [jnp.broadcast_to(placed[m : m + 1, :], (8, 128)) for m in range(8)]
        inverse = [None] * 8
        for k in range(8):
            inverse[k] = 1.0 / a[k, k]
            for i in range(k + 1, 8):
                factor = a[i, k] * inverse[k]
                for q in range(k + 1, i + 1):
                    a[i, q] = a[i, q] - factor * a[q, k]
                lead[i] = lead[i] - factor * lead[k]
                for q in range(k):
                    e[i, q] = e[i, q] - factor * e[k, q]
                e[i, k] = -factor
        scaled = [inverse[m] * lead[m] for m in range(8)]
        solved = list(scaled)
        for m in range(8):
            for n in range(m + 1, 8):
                solved[m] = solved[m] + e[n, m] * scaled[n]
        rows = lead[0] * lax.rsqrt(a[0, 0])
        for m in range(1, 8):
            rows = jnp.where(sub == m, lead[m] * lax.rsqrt(a[m, m]), rows)
        out_ref[first : first + 8, :] = jnp.where(lane <= sub + first, rows, 0.0)
        for i in range(j + 1, count):
            below = blocks[i]
            total = jnp.where(inside, 0.0, below)
            for m in range(8):
                weight = jnp.broadcast_to(below[:, first + m : first + m + 1], (8, 128))
                total = total - weight * solved[m]
            blocks[i] = total


def gather_kernel(
    diag_hbm, panel_hbm, slab_hbm, row_ref, col_ref, slab_ref,
    diag_all, traces, col_all, row_a, row_b, work, inv,
    local_sem, diag_send, diag_recv, rest_send, rest_recv, col_send, col_recv,
    twin_send, twin_recv, part_send, part_recv, one_send, one_recv, two_send, two_recv,
    relay_send, relay_recv,
):
    w, n = lax.axis_index("wide"), lax.axis_index("narrow")
    y, x = lax.div(w, 4), lax.rem(w, 4)
    z, core = lax.div(n, 2), lax.rem(n, 2)

    def piece_at(col, row):
        dx, dy = lax.rem(col + 4 - lax.rem(n, 4), 4), lax.rem(row + 4 - lax.div(n, 4), 4)
        return 4 * lax.rem(dx + dy + z + 2, 4) + dy

    ahead = 1 + 2 * core
    twin = (w, 2 * z + 1 - core)

    def along_x(step):
        return (4 * y + lax.rem(x + step, 4), n)

    def along_y(step):
        return (4 * lax.rem(y + step, 4) + x, n)

    def along_z(step):
        return (w, 2 * lax.rem(z + step, 4) + core)

    def target(half):
        dy = 2 * core + half
        dx = lax.rem(z + 10 - dy - lax.div(w, 2), 4)
        return (4 * lax.rem(y + dy, 4) + lax.rem(x + dx, 4), w)

    source = (n, lax.div(piece_at(x, y), 2))

    slab_copy = pltpu.make_async_copy(slab_hbm, slab_ref, local_sem.at[0])
    diag_own = pltpu.make_async_copy(
        diag_hbm, diag_all.at[pl.ds(pl.multiple_of(32 * n, 32), 32)], local_sem.at[1])
    panel_own = pltpu.make_async_copy(
        panel_hbm, col_all.at[pl.ds(pl.multiple_of(192 * n, 64), 192)], local_sem.at[2])
    diag_own.start()
    panel_own.start()

    barrier = pltpu.get_barrier_semaphore()

    def signal(device):
        pl.semaphore_signal(barrier, inc=1, device_id=device, device_id_type=MESH)

    for step in range(1, 8):
        signal((w, lax.rem(n + step, 8)))
    for step in range(1, 4):
        signal(along_x(step))
        signal(along_y(step))
    signal(source)

    @pl.when(w < 8)
    def _():
        signal(target(0))
        signal(target(1))

    slab_copy.start()
    @pl.when(w < 8)
    def _():
        pl.semaphore_wait(barrier, 16)

    @pl.when(w >= 8)
    def _():
        pl.semaphore_wait(barrier, 14)

    def remote(src, dst, send, recv, device):
        return pltpu.make_async_remote_copy(
            src, dst, send, recv, device_id=device, device_id_type=MESH)

    def corner_copy(step, origin):
        block = diag_all.at[pl.ds(pl.multiple_of(32 * origin, 32), 32), 0:128]
        return remote(block, block, diag_send.at[step], diag_recv.at[origin],
                      (w, lax.rem(n + step, 8)))

    def trace_copy(step, origin):
        return remote(traces.at[origin], traces.at[origin], diag_send.at[step],
                      diag_recv.at[origin], (w, lax.rem(n + step, 8)))

    def rest_copy(step, origin):
        block = diag_all.at[pl.ds(pl.multiple_of(32 * origin, 32), 32)]
        return remote(block, block, rest_send.at[step], rest_recv.at[origin],
                      (w, lax.rem(n + step, 8)))

    line = (y, x)

    def pieces(side, row, first, count):
        start = 192 * row + 48 * first
        return (row_b if side else row_a).at[pl.ds(pl.multiple_of(start, 48), 48 * count)]

    def part_copy(half, side):
        row = lax.rem(target(half)[0], 4) if side else lax.div(target(half)[0], 4)
        return remote(
            col_all.at[pl.ds(pl.multiple_of(192 * n + 96 * half + 48 * side, 48), 48)],
            pieces(side, row, 0, 1), part_send.at[2 * half + side], part_recv.at[side],
            target(half))

    def one_copy(step, side):
        return remote(
            pieces(side, line[side], 0, 1), pieces(side, line[side], 4 - step, 1),
            one_send.at[side, step], one_recv.at[side, step],
            along_y(step) if side else along_x(step))

    def across(step, side):
        return along_x(step) if side else along_y(step)

    def two_copy(step, side, rest):
        block = pieces(side, line[side], 1, 3) if rest else pieces(side, line[side], 0, 1)
        return remote(block, block, two_send.at[side, rest, step], two_recv.at[side, rest, step],
                      across(step, side))

    def relay_copy(side):
        block = pieces(side, lax.rem(line[side] + 4 - ahead, 4), 0, 1)
        return remote(block, block, relay_send.at[side], relay_recv.at[side], across(ahead, side))

    def wait_two(side, forward):
        @pl.when(core == (0 if forward else 1))
        def _():
            two_copy(1, side, 0).wait_recv()

        @pl.when(core == (1 if forward else 0))
        def _():
            two_copy(3, side, 0).wait_recv()

    def col_copy(step):
        block = col_all.at[pl.ds(pl.multiple_of(192 * n, 64), 192)]
        return remote(block, block, col_send.at[step], col_recv.at[step], along_z(step))

    def twin_copy(step):
        origin = 2 * lax.rem(z + 4 - step, 4) + core
        block = col_all.at[pl.ds(pl.multiple_of(192 * origin, 64), 192)]
        return remote(block, block, twin_send.at[step], twin_recv.at[step], twin)

    panel_own.wait()

    @pl.when(w < 8)
    def _():
        for half in range(2):
            for side in range(2):
                part_copy(half, side).start()

    diag_own.wait()
    @pl.when(n < 4)
    def _():
        for step in range(1, 8):
            corner_copy(step, n).start()

    @pl.when(n >= 4)
    def _():
        row_id = lax.broadcasted_iota(jnp.int32, (32, 256), 0)
        col_id = lax.broadcasted_iota(jnp.int32, (32, 256), 1)
        own = diag_all[pl.ds(pl.multiple_of(32 * n, 32), 32), :]
        own = jnp.where(col_id == row_id + 32 * n, own, 0.0)
        own = own[:, 0:128] + own[:, 128:256]
        traces[n] = jnp.sum(own, axis=0, keepdims=True)
        for step in range(1, 8):
            trace_copy(step, n).start()

    @pl.when(n >= 4)
    def _():
        for step in range(1, 8):
            rest_copy(step, n).start()

    def start_cols():
        for step in (1, 3, 2):
            col_copy(step).start()
        twin_copy(0).start()

    def first_phase():
        for side in range(2):
            part_copy(0, side).wait_recv()
            for step in (1, 3, 2):
                one_copy(step, side).start()
            for step in (1, 3):
                two_copy(step, side, 0).start()

    start_cols()
    first_phase()

    for origin in range(4):
        @pl.when(n != origin)
        def _():
            corner_copy(1, origin).wait_recv()
    for origin in range(4, 8):
        @pl.when(n != origin)
        def _():
            trace_copy(1, origin).wait_recv()

    total = jnp.zeros((8, 128), jnp.float32)
    sub = lax.broadcasted_iota(jnp.int32, (8, 128), 0)
    lane = lax.broadcasted_iota(jnp.int32, (8, 128), 1)
    for i in range(16):
        total = total + jnp.where(lane == sub + 8 * i, diag_all[8 * i : 8 * i + 8, 0:128], 0.0)
    total = jnp.sum(total, axis=0, keepdims=True)
    for i in range(4, 8):
        total = total + traces[i]
    shift = unit_gamma * jnp.sum(total, axis=1, keepdims=True) / 256.0

    def shifted(start):
        for i in range(16):
            block = diag_all[start + 8 * i : start + 8 * i + 8, start : start + 128]
            work[start + 8 * i : start + 8 * i + 8, :] = jnp.where(
                lane == sub + 8 * i, block - shift, block)

    def second_phase():
        for side in range(2):
            for step in range(1, 4):
                one_copy(step, side).wait_recv()
            for step in (1, 3, 2):
                two_copy(step, side, 1).start()
        for side in range(2):
            wait_two(side, True)
            relay_copy(side).start()

    def to_twin():
        for step in range(1, 4):
            col_copy(step).wait_recv()
            twin_copy(step).start()

    shifted(0)
    eliminate(work.at[0:128], inv.at[0:128, 0:128], {PHASE_TWO: second_phase})
    inv[0:128, 128:256] = jnp.zeros((128, 128), jnp.float32)
    for origin in range(4, 8):
        @pl.when(n != origin)
        def _():
            rest_copy(1, origin).wait_recv()
    shifted(128)
    first = inv[0:128, 0:128]
    corner = diag_all[128:256, 0:128]
    below = full_dot(corner, first, LAST)
    beside = full_dot(first, corner, LAST)
    work[128:256, :] = work[128:256, :] - full_dot(below, beside, PLAIN)
    eliminate(work.at[128:256], inv.at[128:256, 128:256], {TWIN: to_twin})
    inv[128:256, 0:128] = -full_dot(
        inv[128:256, 128:256], full_dot(below, first, PLAIN), PLAIN)

    inv_high, inv_low = halves(inv[...])

    def solve(raw):
        high, low = halves(raw)
        return halves(half_dot(high, inv_high, LAST) + half_dot(high, inv_low, LAST)
                      + half_dot(low, inv_high, LAST))

    for step in range(4):
        twin_copy(step).wait_recv()
    for start in (0, 768):
        high, low = solve(col_all[start : start + 768, :])
        col_ref[start : start + 768, 0:256] = high
        col_ref[start : start + 768, 256:512] = low
    def place_rows(side, slots, halved):
        for k, (row, step) in enumerate(slots):
            row, other = lax.rem(line[side] + row, 4), lax.rem(line[1 - side] + step, 4)
            place = 96 * (piece_at(row, other) if side else piece_at(other, row)) + 48 * side
            place = pl.ds(pl.multiple_of(place, 48), 48)
            row_ref[place, 0:256] = halved[0][48 * k : 48 * k + 48]
            row_ref[place, 256:512] = halved[1][48 * k : 48 * k + 48]

    early = solve(jnp.concatenate([pieces(side, line[side], 0, 4)[...] for side in range(2)], axis=0))
    for side in range(2):
        rows = slice(192 * side, 192 * side + 192)
        place_rows(side, [(0, j) for j in range(4)], (early[0][rows], early[1][rows]))

    for side in range(2):
        wait_two(side, False)
        relay_copy(side).wait_recv()
        for step in range(1, 4):
            two_copy(step, side, 1).wait_recv()
        late = [pieces(side, lax.rem(line[side] + i, 4), 0, 4)[...] for i in range(1, 4)]
        place_rows(side, [(i, j) for i in range(1, 4) for j in range(4)],
                   solve(jnp.concatenate(late, axis=0)))

    @pl.when(n < 4)
    def _():
        for step in range(1, 8):
            corner_copy(step, n).wait_send()

    @pl.when(n >= 4)
    def _():
        for step in range(1, 8):
            trace_copy(step, n).wait_send()
            rest_copy(step, n).wait_send()

    @pl.when(w < 8)
    def _():
        for half in range(2):
            for side in range(2):
                part_copy(half, side).wait_send()

    for side in range(2):
        for step in range(1, 4):
            one_copy(step, side).wait_send()
            two_copy(step, side, 1).wait_send()
        two_copy(1, side, 0).wait_send()
        two_copy(3, side, 0).wait_send()
        relay_copy(side).wait_send()
    for step in range(1, 4):
        col_copy(step).wait_send()
    for step in range(4):
        twin_copy(step).wait_send()
    slab_copy.wait()


def gather_and_solve(diag_block, panel_below, slab):
    rows = panel_below.shape[0]
    vmem = pl.BlockSpec(memory_space=pltpu.VMEM)
    hbm = pl.BlockSpec(memory_space=pltpu.HBM)
    out = jax.ShapeDtypeStruct((8 * rows, 512), jnp.bfloat16)
    sems = pltpu.SemaphoreType.DMA
    return pl.pallas_call(
        gather_kernel,
        out_shape=(out, out, jax.ShapeDtypeStruct(slab.shape, slab.dtype)),
        in_specs=[hbm, hbm, hbm],
        out_specs=(vmem, vmem, vmem),
        scratch_shapes=[
            pltpu.VMEM((256, 256), jnp.float32),
            pltpu.VMEM((8, 1, 128), jnp.float32),
            pltpu.VMEM((8 * rows, 256), jnp.float32),
            pltpu.VMEM((4 * rows, 256), jnp.float32),
            pltpu.VMEM((4 * rows, 256), jnp.float32),
            pltpu.VMEM((256, 128), jnp.float32),
            pltpu.VMEM((256, 256), jnp.float32),
            sems((3,)), sems((8,)), sems((8,)), sems((8,)), sems((8,)), sems((4,)), sems((4,)),
            sems((4,)), sems((4,)), sems((4,)), sems((2,)), sems((2, 4)), sems((2, 4)),
            sems((2, 2, 4)), sems((2, 2, 4)), sems((2,)), sems((2,)),
        ],
        compiler_params=pltpu.CompilerParams(
            collective_id=0, has_side_effects=True, vmem_limit_bytes=28 << 20),
        name="gather_and_solve",
    )(*(pltpu.with_memory_space_constraint(a, pltpu.HBM) for a in (diag_block, panel_below, slab)))


def update_kernel(row_ref, col_ref, slab_ref, out_hbm, buffer, sem):
    rows, cols = slab_ref.shape
    tall, broad = 384, 512
    copies = []
    for i in range(0, rows, tall):
        for j in range(0, cols, broad):
            t = len(copies)
            high, low = row_ref[i : i + tall, 0:256], row_ref[i : i + tall, 256:512]
            col_high, col_low = col_ref[j : j + broad, 0:256], col_ref[j : j + broad, 256:512]
            product = (half_dot(high, col_high, LAST) + half_dot(high, col_low, LAST)
                       + half_dot(low, col_high, LAST))
            buffer[i : i + tall, j : j + broad] = slab_ref[i : i + tall, j : j + broad] - product
            copies.append(pltpu.make_async_copy(
                buffer.at[pl.ds(i, tall), pl.ds(j, broad)],
                out_hbm.at[pl.ds(i, tall), pl.ds(j, broad)], sem.at[t]))
            copies[-1].start()
    for copy in copies:
        copy.wait()


def update(row_panel, col_panel, slab):
    vmem = pl.BlockSpec(memory_space=pltpu.VMEM)
    return pl.pallas_call(
        update_kernel,
        out_shape=jax.ShapeDtypeStruct(slab.shape, jnp.float32),
        in_specs=[vmem, vmem, vmem],
        out_specs=pl.BlockSpec(memory_space=pltpu.HBM),
        scratch_shapes=[pltpu.VMEM(slab.shape, jnp.float32), pltpu.SemaphoreType.DMA((12,))],
        compiler_params=pltpu.CompilerParams(vmem_limit_bytes=24 << 20),
        name="update",
    )(row_panel, col_panel, slab)


def on_device(diag_block, panel_below, trailing_slab):
    row_panel, col_panel, slab = gather_and_solve(diag_block, panel_below, trailing_slab)
    return update(row_panel, col_panel, slab)


def solution(mesh):
    placed = (P("narrow", None), P(("wide", "narrow"), None), P("narrow", "wide"))
    return jax.shard_map(
        on_device, mesh=mesh, in_specs=placed, out_specs=P("narrow", "wide"), check_vma=False
    )
```
